256 devices in a mesh: robot: 2 (over x_hi), xy: 32 (over y, z), yz: 4 (over x_lo, core).
Axes of the slice: x: 4 (x_hi: 2, x_lo: 2; x = x_hi * 2 + x_lo), y: 4, z: 8, core: 2. Of those that a mesh axis runs over, the one named last changes fastest.
Arguments:
- seed_cost: bfloat16 [4, 64, 512, 512], P('robot', None, 'xy', 'yz'), may hold values from 0 to 9
- occupied: int32 [64, 512, 512], P(None, 'xy', 'yz'), may hold values from 0 to 1, as said below
- unknown: int32 [64, 512, 512], P(None, 'xy', 'yz'), may hold values from 0 to 1, as said below
Outputs:
- signed: float32 [64, 512, 512], P(('robot', 'xy'), 'yz')
The draws below stay inside these ranges and needn't reach their ends.
Inputs may be any that keep to these rules, and one draw needn't show every extreme that they name: At least one cell is occupied. At least one cell is neither occupied nor unknown.
All inputs are finite; a program needn't handle non-finite values.
Results may differ from the reference program's by a relative error of at most 0.0003.
Values may be sent and summed in bfloat16 or wider, within the bound.
No kernel may reach another device: no remote copies, remote signals or barrier semaphores. Data moves between devices by JAX's collectives and lax.ppermute only.
A program may use at most 64 MiB of HBM per device.

```python
import jax
import jax.numpy as jnp
from jax import lax

NX = 512
NY = 512
NZ = 64
ROBOTS = 4


def inside_range(places, low, high):
    return (places >= low) & (places < high)


def box_mask(depth_part, row_part, column_part):
    return depth_part[:, None, None] & row_part[None, :, None] & column_part[None, None, :]


def draw_occupied(key, part):
    base = jax.random.fold_in(key, 7301)
    depth_index = jnp.arange(NZ, dtype=jnp.int32)
    row_index = jnp.arange(NX, dtype=jnp.int32)
    column_index = jnp.arange(NY, dtype=jnp.int32)
    filled = jnp.zeros((NZ, NX, NY), dtype=jnp.bool_)
    for wall_number in range(8):
        sub_keys = jax.random.split(jax.random.fold_in(base, wall_number), 8)
        facing = jax.random.randint(sub_keys[0], (), 0, 2)
        place_row = jax.random.randint(sub_keys[1], (), 0, NX)
        place_column = jax.random.randint(sub_keys[2], (), 0, NY)
        start_row = jax.random.randint(sub_keys[3], (), 0, NX)
        start_column = jax.random.randint(sub_keys[4], (), 0, NY)
        length_row = jax.random.randint(sub_keys[5], (), NX // 8, NX // 2 + 1)
        length_column = jax.random.randint(sub_keys[6], (), NY // 8, NY // 2 + 1)
        height = jax.random.randint(sub_keys[7], (), NZ // 2, NZ + 1)
        rows_part = jnp.where(facing == 0, inside_range(row_index, place_row, place_row + 1), inside_range(row_index, start_row, start_row + length_row))
        columns_part = jnp.where(facing == 0, inside_range(column_index, start_column, start_column + length_column), inside_range(column_index, place_column, place_column + 1))
        depths_part = inside_range(depth_index, 0, height)
        filled = filled | box_mask(depths_part, rows_part, columns_part)
    for object_number in range(3):
        sub_keys = jax.random.split(jax.random.fold_in(base, 100 + object_number), 6)
        low_depth = jax.random.randint(sub_keys[0], (), 0, NZ)
        side_depth = jax.random.randint(sub_keys[1], (), 2, 17)
        low_row = jax.random.randint(sub_keys[2], (), 0, NX)
        side_row = jax.random.randint(sub_keys[3], (), 2, 17)
        low_column = jax.random.randint(sub_keys[4], (), 0, NY)
        side_column = jax.random.randint(sub_keys[5], (), 2, 17)
        filled = filled | box_mask(inside_range(depth_index, low_depth, low_depth + side_depth), inside_range(row_index, low_row, low_row + side_row), inside_range(column_index, low_column, low_column + side_column))
    return filled.astype(jnp.int32)


def draw_unknown(key, part):
    base = jax.random.fold_in(key, 9203)
    depth_index = jnp.arange(NZ, dtype=jnp.int32)
    row_index = jnp.arange(NX, dtype=jnp.int32)
    column_index = jnp.arange(NY, dtype=jnp.int32)
    region = jnp.zeros((NZ, NX, NY), dtype=jnp.bool_)
    for region_number in range(2):
        sub_keys = jax.random.split(jax.random.fold_in(base, region_number), 5)
        low_row = jax.random.randint(sub_keys[0], (), 0, NX)
        side_row = jax.random.randint(sub_keys[1], (), NX // 4, 3 * NX // 4 + 1)
        low_column = jax.random.randint(sub_keys[2], (), 0, NY)
        side_column = jax.random.randint(sub_keys[3], (), NY // 4, 3 * NY // 4 + 1)
        height = jax.random.randint(sub_keys[4], (), NZ // 2, 3 * NZ // 4 + 1)
        region = region | box_mask(inside_range(depth_index, 0, height), inside_range(row_index, low_row, low_row + side_row), inside_range(column_index, low_column, low_column + side_column))
    speckle = jax.random.randint(jax.random.fold_in(base, 50), (NZ, NX, NY), 0, 16) == 0
    return (region | speckle).astype(jnp.int32)


def block_levels(stream_key, shape, shards, low, high):
    def one(axis_at, blocks):
        draws = jax.random.uniform(jax.random.fold_in(jax.random.fold_in(stream_key, 6), axis_at), (blocks,), jnp.float32, low / len(shards), high / len(shards))
        return jnp.repeat(jnp.exp(draws), shape[axis_at] // blocks).reshape((-1,) + (1,) * (len(shape) - axis_at - 1))

    loudness = one(*shards[0])
    for cut in shards[1:]:
        loudness = loudness * one(*cut)
    return loudness


def setup_inputs(seed: int = 0) -> dict:
    key_of = jax.random.split(jax.random.key(seed), 4)
    seed_cost = jnp.clip(9.0 * jax.random.uniform(key_of[0], (ROBOTS, NZ, NX, NY), jnp.float32) ** block_levels(key_of[0], (ROBOTS, NZ, NX, NY), ((0, 2), (2, 32), (3, 4)), -0.2, 0.2), 0.0, 9.0).astype(jnp.bfloat16)
    occupied = draw_occupied(jax.random.fold_in(key_of[3], 71), 0)
    unknown = draw_unknown(jax.random.fold_in(key_of[3], 71), 0)
    return {"seed_cost": seed_cost, "occupied": occupied, "unknown": unknown}


penalty = 1048576.0
voxel_size = 0.2

def lower_envelope(values, along):
    extent = values.shape[along]
    block_size = min(extent, 128)
    places = jnp.arange(extent, dtype=jnp.float32)
    pieces = []
    for offset in range(0, extent, block_size):
        target = places[offset:offset + block_size]
        table = (places[:, None] - target[None, :]) ** 2
        layout = [1] * (values.ndim + 1)
        layout[along] = extent
        layout[along + 1] = block_size
        summed = jnp.expand_dims(values, along + 1) + table.reshape(layout)
        pieces.append(lax.optimization_barrier(jnp.min(summed, axis=along)))
    return jnp.concatenate(pieces, axis=along)

def depth_pass(layer_plane):
    return lower_envelope(layer_plane, 0)

def column_pass(layer_plane):
    return lower_envelope(layer_plane, 1)

def three_passes(field):
    field = jnp.transpose(lax.map(depth_pass, jnp.transpose(field, (1, 0, 2))), (1, 0, 2))
    field = lax.map(depth_pass, field)
    field = lax.map(column_pass, field)
    return field

def reference(seed_cost, occupied, unknown):
    merged = lax.optimization_barrier(jnp.min(seed_cost, axis=0))
    merged_cost = merged.astype(jnp.float32)
    outside = jnp.where(occupied == 1, merged_cost, merged_cost + penalty)
    inside = jnp.where((occupied == 1) | (unknown == 1), merged_cost + penalty, merged_cost)
    far_out = three_passes(outside)
    far_in = three_passes(inside)
    return voxel_size * (jnp.sqrt(far_out) - jnp.sqrt(far_in))
```

```python
import jax
import jax.numpy as jnp
from jax import lax
from jax.experimental import pallas as pl
from jax.experimental.pallas import tpu as pltpu
from jax.sharding import PartitionSpec as P

penalty = 1048576.0
voxel_size = 0.2

LANES = 128
ROWS = 8
LINE = 512
BLOCK = 32
BLOCKS = LINE // BLOCK
GROUPS = BLOCK // ROWS
FIELDS = 2
MIDDLE = 64


def depth_kernel(half_ref, mine_ref, other_ref, occupied_ref, unknown_ref, out_ref, field_ref):
    half = half_ref[0]
    depth = mine_ref.shape[0]
    own = out_ref.shape[0]

    def seed(place, _):
        source = place + half * (depth - 1 - 2 * place)
        merged = jnp.minimum(mine_ref[source], other_ref[source]).astype(jnp.float32)
        taken = occupied_ref[source] == 1
        hidden = taken | (unknown_ref[source] == 1)
        raised = merged + penalty
        field_ref[0, place] = jnp.where(taken, merged, raised)
        field_ref[1, place] = jnp.where(hidden, raised, merged)
        return 0

    lax.fori_loop(0, depth, seed, 0, unroll=4)
    groups = field_ref.shape[2] // ROWS

    def sweep(piece, _):
        field = piece // groups
        rows = pl.ds(pl.multiple_of((piece - field * groups) * ROWS, ROWS), ROWS)
        best = [None] * own
        for source in range(depth):
            value = field_ref[field, source, rows, :]
            for target in range(own):
                candidate = value + float((target - source) ** 2)
                best[target] = candidate if best[target] is None else jnp.minimum(best[target], candidate)
        for target in range(own):
            out_ref[target + half * (own - 1 - 2 * target), field, rows, :] = best[target]
        return 0

    lax.fori_loop(0, FIELDS * groups, sweep, 0)


def fill_table(table_ref):
    sublane = lax.broadcasted_iota(jnp.int32, (ROWS, LANES), 0).astype(jnp.float32)

    def step(k, _):
        base = sublane + (ROWS * (k - MIDDLE)).astype(jnp.float32)
        for p in range(ROWS):
            apart = base - float(p)
            table_ref[p, k] = apart * apart
        return 0

    lax.fori_loop(0, 2 * MIDDLE, step, 0, unroll=4)


def find_blocks(load, found_ref):
    sublane = lax.broadcasted_iota(jnp.int32, (ROWS, LANES), 0).astype(jnp.float32)
    for field in range(FIELDS):
        low = []
        for block in range(BLOCKS):
            least = load(field, block * BLOCK)
            for group in range(1, GROUPS):
                least = jnp.minimum(least, load(field, block * BLOCK + group * ROWS))
            low.append(jnp.broadcast_to(jnp.min(least, axis=0, keepdims=True), (ROWS, LANES)))
        for first in range(0, BLOCKS, ROWS):
            bound = None
            floor = []
            for block in range(BLOCKS):
                away = jnp.abs(sublane + float(first - block)) * float(BLOCK)
                far = away + float(BLOCK - 1)
                near = jnp.maximum(away - float(BLOCK - 1), 0.0)
                upper = low[block] + far * far
                bound = upper if bound is None else jnp.minimum(bound, upper)
                floor.append(low[block] + near * near)
            count = jnp.zeros((ROWS, 1), jnp.int32)
            words = [count, count]
            for block in range(BLOCKS):
                keep = jnp.min(floor[block] - bound, axis=1, keepdims=True) < 0.0
                code = lax.shift_left(jnp.full((ROWS, 1), block, jnp.int32), (count & 7) * 4)
                words[0] = words[0] | jnp.where(keep & (count < 8), code, 0)
                words[1] = words[1] | jnp.where(keep & (count >= 8), code, 0)
                count = count + jnp.where(keep, 1, 0)
            place = field * BLOCKS + first
            for which, value in enumerate((count, *words)):
                found_ref[which, place : place + ROWS, :] = jnp.broadcast_to(value, (ROWS, LANES))


def line_pass(load, load_row, store, table_ref, found_ref, list_ref, sem):
    fill_table(table_ref)
    find_blocks(load, found_ref)
    copy = pltpu.make_async_copy(found_ref, list_ref, sem)
    copy.start()
    copy.wait()

    def target(place, _):
        field = place // BLOCKS
        block = place - field * BLOCKS

        def pair(_, carry):
            low_word, high_word, best = carry
            source = low_word & 15
            low_word = lax.shift_right_logical(low_word, 4) | lax.shift_left(high_word & 15, 28)
            high_word = lax.shift_right_logical(high_word, 4)
            base = (block - source) * GROUPS + MIDDLE
            best = list(best)
            for p in range(ROWS):
                squares = {k: table_ref[p, base + k] for k in range(1 - GROUPS, GROUPS)}
                for q in range(GROUPS):
                    value = jnp.broadcast_to(load_row(field, source, q * ROWS + p), (ROWS, LANES))
                    for group in range(GROUPS):
                        best[group] = jnp.minimum(best[group], value + squares[group - q])
            return low_word, high_word, tuple(best)

        start = jnp.full((ROWS, LANES), 3e38, jnp.float32)
        state = (list_ref[1, place, 0], list_ref[2, place, 0], (start,) * GROUPS)
        best = lax.fori_loop(0, list_ref[0, place, 0], pair, state)[2]
        for group in range(GROUPS):
            store(field, block, group, best[group])
        return 0

    lax.fori_loop(0, FIELDS * BLOCKS, target, 0)


def row_kernel(in_ref, out_ref, table_ref, found_ref, list_ref, sem):
    chunk = in_ref.shape[2]
    per_block = BLOCK // chunk
    per_out = out_ref.shape[2] // BLOCK

    def load(field, at):
        return in_ref[at // chunk, field, pl.ds(at % chunk, ROWS), :]

    def load_row(field, block, at):
        return in_ref[block * per_block + at // chunk, field, pl.ds(at % chunk, 1), :]

    def store(field, block, group, value):
        piece = block // per_out
        at = pl.multiple_of((block - piece * per_out) * BLOCK, BLOCK) + group * ROWS
        out_ref[piece, field, pl.ds(at, ROWS), :] = value

    line_pass(load, load_row, store, table_ref, found_ref, list_ref, sem)


def column_kernel(in_ref, out_ref, line_ref, far_ref, table_ref, found_ref, list_ref, sem):
    pieces = in_ref.shape[0]
    for piece in range(pieces):
        for field in range(FIELDS):
            line_ref[field, piece * LANES : (piece + 1) * LANES, :] = in_ref[piece, field].T

    def load(field, at):
        return line_ref[field, pl.ds(at, ROWS), :]

    def load_row(field, block, at):
        return line_ref[field, pl.ds(pl.multiple_of(block * BLOCK, BLOCK) + at, 1), :]

    def store(field, block, group, value):
        at = pl.multiple_of(block * BLOCK, BLOCK) + group * ROWS
        far_ref[field, pl.ds(at, ROWS), :] = value

    line_pass(load, load_row, store, table_ref, found_ref, list_ref, sem)
    for piece in range(pieces):
        part = pl.ds(piece * LANES, LANES)
        signed = voxel_size * (jnp.sqrt(far_ref[0, part, :]) - jnp.sqrt(far_ref[1, part, :]))
        out_ref[:, part] = signed.T


def line_scratch():
    return [
        pltpu.VMEM((ROWS, 2 * MIDDLE, ROWS, LANES), jnp.float32),
        pltpu.VMEM((3, FIELDS * BLOCKS, LANES), jnp.int32),
        pltpu.SMEM((3, FIELDS * BLOCKS, LANES), jnp.int32),
        pltpu.SemaphoreType.DMA,
    ]


def body(seed_cost, occupied, unknown):
    depth, rows, columns = occupied.shape
    own = depth // lax.axis_size("robot")
    params = pltpu.CompilerParams(vmem_limit_bytes=32 * 2**20)
    vmem = pl.BlockSpec(memory_space=pltpu.VMEM)
    lowest = jnp.min(seed_cost, axis=0)
    other = lax.ppermute(lowest, "robot", [(0, 1), (1, 0)])
    half = lax.axis_index("robot").astype(jnp.int32).reshape(1)
    planes = pl.pallas_call(
        depth_kernel,
        out_shape=jax.ShapeDtypeStruct((own, FIELDS, rows, columns), jnp.float32),
        in_specs=[pl.BlockSpec(memory_space=pltpu.SMEM)] + [vmem] * 4,
        out_specs=vmem,
        scratch_shapes=[pltpu.VMEM((FIELDS, depth, rows, columns), jnp.float32)],
        compiler_params=params,
    )(half, lowest, other, occupied, unknown)
    crossed = lax.all_to_all(planes, "xy", split_axis=0, concat_axis=0, tiled=True)
    parts = lax.axis_size("yz")
    share = LINE // parts
    settled = pl.pallas_call(
        row_kernel,
        out_shape=jax.ShapeDtypeStruct((parts, FIELDS, share, columns), jnp.float32),
        in_specs=[vmem],
        out_specs=vmem,
        scratch_shapes=line_scratch(),
        compiler_params=params,
    )(crossed)
    turned = lax.all_to_all(settled, "yz", split_axis=0, concat_axis=0, tiled=True)
    signed = pl.pallas_call(
        column_kernel,
        out_shape=jax.ShapeDtypeStruct((share, LINE), jnp.float32),
        in_specs=[vmem],
        out_specs=vmem,
        scratch_shapes=[pltpu.VMEM((FIELDS, LINE, share), jnp.float32)] * 2 + line_scratch(),
        compiler_params=params,
    )(turned)
    return signed[None]


def solution(mesh):
    in_specs = (P("robot", None, "xy", "yz"), P(None, "xy", "yz"), P(None, "xy", "yz"))
    out_specs = P(("robot", "xy"), "yz", None)
    return jax.shard_map(body, mesh=mesh, in_specs=in_specs, out_specs=out_specs, check_vma=False)
```

```python
import functools

import jax
import jax.numpy as jnp
from jax import lax
from jax.experimental import pallas as pl
from jax.experimental.pallas import tpu as pltpu
from jax.sharding import PartitionSpec as P

penalty = 1048576.0
voxel_size = 0.2

LANES = 128
ROWS = 8
LINE = 512
BLOCK = 32
BLOCKS = LINE // BLOCK
GROUPS = BLOCK // ROWS
FIELDS = 2
MIDDLE = 64

STEPS = 65520.0 / 13.8629653
HALF_RANGE = 32768


def encode(value):
    code = (jnp.log(1.0 + value) * STEPS + 0.5).astype(jnp.int32)
    return (code - HALF_RANGE).astype(jnp.int16)


def decode(code):
    scaled = (code.astype(jnp.int32) + HALF_RANGE).astype(jnp.float32) * (1.0 / STEPS)
    return jnp.maximum(jnp.exp(scaled) - 1.0, 0.0)


def prepare_kernel(occupied_ref, unknown_ref, raise_ref):
    def masks(place, _):
        taken = occupied_ref[place] == 1
        hidden = taken | (unknown_ref[place] == 1)
        raise_ref[0, place] = jnp.where(taken, 0.0, penalty)
        raise_ref[1, place] = jnp.where(hidden, penalty, 0.0)
        return 0

    lax.fori_loop(0, occupied_ref.shape[0], masks, 0, unroll=4)


def depth_kernel(half_ref, mine_ref, other_ref, raise_ref, out_ref, field_ref, best_ref):
    half = half_ref[0]
    depth = mine_ref.shape[0]
    own = out_ref.shape[0]

    def seed(place, _):
        source = place + half * (depth - 1 - 2 * place)
        merged = jnp.minimum(mine_ref[source], other_ref[source]).astype(jnp.float32)
        for field in range(FIELDS):
            field_ref[field, place] = merged + raise_ref[field, source]
        return 0

    lax.fori_loop(0, depth, seed, 0, unroll=4)
    groups = field_ref.shape[2] // ROWS

    def sweep(piece, _):
        field = piece // groups
        rows = pl.ds(pl.multiple_of((piece - field * groups) * ROWS, ROWS), ROWS)
        best = [None] * own
        for source in range(depth):
            value = field_ref[field, source, rows, :]
            for target in range(own):
                candidate = value + float((target - source) ** 2)
                best[target] = candidate if best[target] is None else jnp.minimum(best[target], candidate)
        for target in range(own):
            best_ref[field, target, rows, :] = best[target]
        return 0

    lax.fori_loop(0, FIELDS * groups, sweep, 0)

    def send(target, _):
        place = target + half * (own - 1 - 2 * target)
        for field in range(FIELDS):
            out_ref[place, field] = encode(best_ref[field, target])
        return 0

    lax.fori_loop(0, own, send, 0, unroll=4)


def fill_table(table_ref):
    sublane = lax.broadcasted_iota(jnp.int32, (ROWS, LANES), 0).astype(jnp.float32)

    def squares(k, _):
        base = sublane + (ROWS * (k - MIDDLE)).astype(jnp.float32)
        for p in range(ROWS):
            apart = base - float(p)
            table_ref[p, k] = apart * apart
        return 0

    lax.fori_loop(0, 2 * MIDDLE, squares, 0, unroll=4)


def find_blocks(line_ref, kept_ref):
    sublane = lax.broadcasted_iota(jnp.int32, (ROWS, LANES), 0).astype(jnp.float32)
    low = []
    for block in range(BLOCKS):
        least = line_ref[block * BLOCK : block * BLOCK + ROWS, :]
        for group in range(1, GROUPS):
            at = block * BLOCK + group * ROWS
            least = jnp.minimum(least, line_ref[at : at + ROWS, :])
        low.append(jnp.broadcast_to(jnp.min(least, axis=0, keepdims=True), (ROWS, LANES)))
    for first in range(0, BLOCKS, ROWS):
        bound = None
        floor = []
        for block in range(BLOCKS):
            away = jnp.abs(sublane + float(first - block)) * float(BLOCK)
            far = away + float(BLOCK - 1)
            near = jnp.maximum(away - float(BLOCK - 1), 0.0)
            upper = low[block] + far * far
            bound = upper if bound is None else jnp.minimum(bound, upper)
            floor.append(low[block] + near * near)
        kept = jnp.zeros((ROWS, 1), jnp.int32)
        for block in range(BLOCKS):
            keep = jnp.min(floor[block] - bound, axis=1, keepdims=True) < 0.0
            kept = kept | jnp.where(keep, 1 << block, 0)
        for row in range(ROWS):
            kept_ref[first + row] = kept[row, 0]


def line_pass(line_ref, far_ref, table_ref, kept_ref):
    find_blocks(line_ref, kept_ref)

    def target(block, _):
        def left(carry):
            return carry[0] != 0

        def pair(carry):
            kept, best = carry
            source = 31 - lax.clz(kept)
            kept = kept ^ lax.shift_left(jnp.int32(1), source)
            base = (block - source) * GROUPS + MIDDLE
            row = pl.multiple_of(source * BLOCK, BLOCK)
            best = list(best)
            for p in range(ROWS):
                squares = {k: table_ref[p, base + k] for k in range(1 - GROUPS, GROUPS)}
                for q in range(GROUPS):
                    value = jnp.broadcast_to(line_ref[pl.ds(row + q * ROWS + p, 1), :], (ROWS, LANES))
                    for group in range(GROUPS):
                        best[group] = jnp.minimum(best[group], value + squares[group - q])
            return kept, tuple(best)

        start = jnp.full((ROWS, LANES), 3e38, jnp.float32)
        best = lax.while_loop(left, pair, (kept_ref[block], (start,) * GROUPS))[1]
        at = pl.multiple_of(block * BLOCK, BLOCK)
        for group in range(GROUPS):
            far_ref[pl.ds(at + group * ROWS, ROWS), :] = best[group]
        return 0

    lax.fori_loop(0, BLOCKS, target, 0)


def row_kernel(field, me_ref, in_ref, *rest):
    (table_ref, own_ref, *send_refs), (line_ref, far_ref, kept_ref) = rest[:-3], rest[-3:]
    if field == 0:
        fill_table(table_ref)
    chunk = in_ref.shape[2]
    for piece in range(in_ref.shape[0]):
        line_ref[piece * chunk : (piece + 1) * chunk, :] = decode(in_ref[piece, field])
    line_pass(line_ref, far_ref, table_ref, kept_ref)
    for step in range(len(send_refs) + 1):
        part = pl.ds(pl.multiple_of((me_ref[0] ^ step) * LANES, LANES), LANES)
        value = far_ref[part, :].T
        if step:
            send_refs[step - 1][...] = encode(value)
        else:
            own_ref[...] = value


def gather_lines(me_ref, own_ref, got_refs, line_ref):
    for step in range(len(got_refs) + 1):
        part = pl.ds(pl.multiple_of((me_ref[0] ^ step) * LANES, LANES), LANES)
        line_ref[part, :] = decode(got_refs[step - 1][...]) if step else own_ref[...]


def column_kernel(me_ref, table_ref, own_ref, *rest):
    got_refs, (far_ref, line_ref, kept_ref) = rest[:-3], rest[-3:]
    gather_lines(me_ref, own_ref, got_refs, line_ref)
    line_pass(line_ref, far_ref, table_ref, kept_ref)


def last_kernel(me_ref, table_ref, outside_ref, own_ref, *rest):
    got_refs, (out_ref, line_ref, far_ref, kept_ref) = rest[:-4], rest[-4:]
    gather_lines(me_ref, own_ref, got_refs, line_ref)
    line_pass(line_ref, far_ref, table_ref, kept_ref)
    for piece in range(LINE // LANES):
        part = pl.ds(piece * LANES, LANES)
        signed = voxel_size * (jnp.sqrt(outside_ref[part, :]) - jnp.sqrt(far_ref[part, :]))
        out_ref[:, part] = signed.T


def body(seed_cost, occupied, unknown):
    depth, rows, columns = occupied.shape
    own = depth // lax.axis_size("robot")
    vmem = pl.BlockSpec(memory_space=pltpu.VMEM)
    smem = pl.BlockSpec(memory_space=pltpu.SMEM)
    f32 = jnp.float32

    def call(kernel, out_shape, scratch, *args, scalar=False, work=4e6):
        in_specs = [smem if scalar and n == 0 else vmem for n in range(len(args))]
        return pl.pallas_call(
            kernel,
            out_shape=out_shape,
            in_specs=in_specs,
            out_specs=jax.tree.map(lambda _: vmem, out_shape),
            scratch_shapes=scratch,
            compiler_params=pltpu.CompilerParams(vmem_limit_bytes=16 * 2**20),
            cost_estimate=pl.CostEstimate(flops=int(work), bytes_accessed=2**20, transcendentals=0),
        )(*args)

    lowest = jnp.min(seed_cost, axis=0)
    other = lax.ppermute(lowest, "robot", [(0, 1), (1, 0)])
    raised = call(
        prepare_kernel, jax.ShapeDtypeStruct((FIELDS, depth, rows, columns), f32), [], occupied, unknown
    )
    half = lax.axis_index("robot").astype(jnp.int32).reshape(1)
    planes = call(
        depth_kernel,
        jax.ShapeDtypeStruct((own, FIELDS, rows, columns), jnp.int16),
        [pltpu.VMEM((FIELDS, depth, rows, columns), f32), pltpu.VMEM((FIELDS, own, rows, columns), f32)],
        half,
        lowest,
        other,
        raised,
        scalar=True,
    )
    crossed = lax.all_to_all(planes, "xy", split_axis=0, concat_axis=0, tiled=True)

    parts = lax.axis_size("yz")
    share = LINE // parts
    me = lax.axis_index("yz").astype(jnp.int32).reshape(1)
    line = pltpu.VMEM((LINE, LANES), f32)
    kept = pltpu.SMEM((BLOCKS,), jnp.int32)
    shapes = (jax.ShapeDtypeStruct((columns, share), f32),)
    shapes += (jax.ShapeDtypeStruct((columns, share), jnp.int16),) * (parts - 1)
    squares = jax.ShapeDtypeStruct((ROWS, 2 * MIDDLE, ROWS, LANES), f32)
    scratch = [line, line, kept]
    row_calls = [functools.partial(row_kernel, field) for field in range(FIELDS)]
    table, *first = call(row_calls[0], (squares, *shapes), scratch, me, crossed, scalar=True)
    second = call(row_calls[1], shapes, scratch, me, crossed, table, scalar=True)
    settled = []
    for made in (first, second):
        got = [
            lax.ppermute(made[step], "yz", [(i, i ^ step) for i in range(parts)]) for step in range(1, parts)
        ]
        settled.append((made[0], *got))
    outside = call(
        column_kernel, jax.ShapeDtypeStruct((LINE, share), f32), [line, kept], me, table, *settled[0], scalar=True
    )
    signed = call(
        last_kernel,
        jax.ShapeDtypeStruct((share, LINE), f32),
        [line, line, kept],
        me,
        table,
        outside,
        *settled[1],
        scalar=True,
    )
    return signed[None]


def solution(mesh):
    in_specs = (P("robot", None, "xy", "yz"), P(None, "xy", "yz"), P(None, "xy", "yz"))
    out_specs = P(("robot", "xy"), "yz", None)
    return jax.shard_map(body, mesh=mesh, in_specs=in_specs, out_specs=out_specs, check_vma=False)
```

```python
import functools

import jax
import jax.numpy as jnp
from jax import lax
from jax.experimental import pallas as pl
from jax.experimental.pallas import tpu as pltpu
from jax.sharding import PartitionSpec as P

penalty = 1048576.0
voxel_size = 0.2

LANES = 128
ROWS = 8
LINE = 512
BLOCK = 32
BLOCKS = LINE // BLOCK
GROUPS = BLOCK // ROWS
FIELDS = 2

STEPS = 65520.0 / 13.8629653
HALF_RANGE = 32768


def encode(value):
    code = (jnp.log(1.0 + value) * STEPS + 0.5).astype(jnp.int32)
    return (code - HALF_RANGE).astype(jnp.int16)


def decode(code):
    scaled = (code.astype(jnp.int32) + HALF_RANGE).astype(jnp.float32) * (1.0 / STEPS)
    return jnp.maximum(jnp.exp(scaled) - 1.0, 0.0)


def prepare_kernel(occupied_ref, unknown_ref, raise_ref):
    def masks(place, _):
        taken = occupied_ref[place] == 1
        hidden = taken | (unknown_ref[place] == 1)
        raise_ref[0, place] = jnp.where(taken, 0.0, penalty)
        raise_ref[1, place] = jnp.where(hidden, penalty, 0.0)
        return 0

    lax.fori_loop(0, occupied_ref.shape[0], masks, 0, unroll=4)


def depth_kernel(place_ref, mine_ref, other_ref, raise_ref, out_ref, field_ref, best_ref):
    half = place_ref[0]
    depth = mine_ref.shape[0]
    own = out_ref.shape[0]

    def seed(place, _):
        source = place + half * (depth - 1 - 2 * place)
        merged = jnp.minimum(mine_ref[source], other_ref[source]).astype(jnp.float32)
        for field in range(FIELDS):
            field_ref[field, place] = merged + raise_ref[field, source]
        return 0

    lax.fori_loop(0, depth, seed, 0, unroll=4)
    groups = field_ref.shape[2] // ROWS

    def sweep(piece, _):
        field = piece // groups
        rows = pl.ds(pl.multiple_of((piece - field * groups) * ROWS, ROWS), ROWS)
        best = [None] * own
        for source in range(depth):
            value = field_ref[field, source, rows, :]
            for target in range(own):
                candidate = value + float((target - source) ** 2)
                best[target] = candidate if best[target] is None else jnp.minimum(best[target], candidate)
        for target in range(own):
            best_ref[field, target, rows, :] = best[target]
        return 0

    lax.fori_loop(0, FIELDS * groups, sweep, 0)

    def send(target, _):
        place = target + half * (own - 1 - 2 * target)
        for field in range(FIELDS):
            out_ref[place, field] = encode(best_ref[field, target])
        return 0

    lax.fori_loop(0, own, send, 0, unroll=4)


def find_blocks(line_ref, kept_ref):
    sublane = lax.broadcasted_iota(jnp.int32, (ROWS, LANES), 0).astype(jnp.float32)
    low = []
    for block in range(BLOCKS):
        least = line_ref[block * BLOCK : block * BLOCK + ROWS, :]
        for group in range(1, GROUPS):
            at = block * BLOCK + group * ROWS
            least = jnp.minimum(least, line_ref[at : at + ROWS, :])
        low.append(jnp.broadcast_to(jnp.min(least, axis=0, keepdims=True), (ROWS, LANES)))
    for first in range(0, BLOCKS, ROWS):
        bound = jnp.full((ROWS, LANES), penalty, jnp.float32)
        floor = []
        for block in range(BLOCKS):
            away = jnp.abs(sublane + float(first - block)) * float(BLOCK)
            far = away + float(BLOCK - 1)
            near = jnp.maximum(away - float(BLOCK - 1), 0.0)
            bound = jnp.minimum(bound, low[block] + far * far)
            floor.append(low[block] + near * near)
        kept = jnp.zeros((ROWS, 1), jnp.int32)
        for block in range(BLOCKS):
            keep = jnp.min(floor[block] - bound, axis=1, keepdims=True) < 0.0
            kept = kept | jnp.where(keep, 1 << block, 0)
        for row in range(ROWS):
            kept_ref[first + row] = kept[row, 0]


def line_pass(line_ref, far_ref, table_ref, kept_ref):
    sublane = lax.broadcasted_iota(jnp.int32, (ROWS, LANES), 0).astype(jnp.float32)
    for at in range(0, 2 * LINE, ROWS):
        apart = sublane + float(at - LINE)
        table_ref[at : at + ROWS, :] = apart * apart
    find_blocks(line_ref, kept_ref)

    def target(block, _):
        at = pl.multiple_of(block * BLOCK, BLOCK)

        def left(carry):
            return carry[0] != 0

        def pair(carry):
            kept, source, best = carry
            base = pl.multiple_of((block - source) * BLOCK + LINE, BLOCK)
            row = pl.multiple_of(source * BLOCK, BLOCK)
            kept = kept ^ lax.shift_left(jnp.int32(1), source)
            best = list(best)
            for p in range(ROWS):
                squares = {k: table_ref[pl.ds(base + (k * ROWS - p), ROWS), :] for k in range(1 - GROUPS, GROUPS)}
                for q in range(GROUPS):
                    value = jnp.broadcast_to(line_ref[pl.ds(row + q * ROWS + p, 1), :], (ROWS, LANES))
                    for group in range(GROUPS):
                        best[group] = jnp.minimum(best[group], value + squares[group - q])
            return kept, 31 - lax.clz(kept), tuple(best)

        kept = kept_ref[block]
        start = tuple(line_ref[pl.ds(at + group * ROWS, ROWS), :] for group in range(GROUPS))
        best = lax.while_loop(left, pair, (kept, 31 - lax.clz(kept), start))[2]
        for group in range(GROUPS):
            far_ref[pl.ds(at + group * ROWS, ROWS), :] = best[group]
        return 0

    lax.fori_loop(0, BLOCKS, target, 0)


def row_kernel(field, place_ref, in_ref, own_ref, *rest):
    send_refs, (line_ref, far_ref, table_ref, kept_ref) = rest[:-4], rest[-4:]
    chunk = in_ref.shape[2]
    for piece in range(in_ref.shape[0]):
        line_ref[piece * chunk : (piece + 1) * chunk, :] = decode(in_ref[piece, field])
    line_pass(line_ref, far_ref, table_ref, kept_ref)
    for step in range(len(send_refs) + 1):
        part = pl.ds(pl.multiple_of((place_ref[1] ^ step) * LANES, LANES), LANES)
        value = far_ref[part, :].T
        if step:
            send_refs[step - 1][...] = encode(value)
        else:
            own_ref[...] = value


def gather_lines(place_ref, own_ref, got_refs, line_ref):
    for step in range(len(got_refs) + 1):
        part = pl.ds(pl.multiple_of((place_ref[1] ^ step) * LANES, LANES), LANES)
        line_ref[part, :] = decode(got_refs[step - 1][...]) if step else own_ref[...]


def column_kernel(place_ref, own_ref, *rest):
    got_refs, (far_ref, line_ref, table_ref, kept_ref) = rest[:-4], rest[-4:]
    gather_lines(place_ref, own_ref, got_refs, line_ref)
    line_pass(line_ref, far_ref, table_ref, kept_ref)


def last_kernel(place_ref, outside_ref, own_ref, *rest):
    got_refs, (out_ref, line_ref, far_ref, table_ref, kept_ref) = rest[:-5], rest[-5:]
    gather_lines(place_ref, own_ref, got_refs, line_ref)
    line_pass(line_ref, far_ref, table_ref, kept_ref)
    for piece in range(LINE // LANES):
        part = pl.ds(piece * LANES, LANES)
        signed = voxel_size * (jnp.sqrt(outside_ref[part, :]) - jnp.sqrt(far_ref[part, :]))
        out_ref[:, part] = signed.T


def body(seed_cost, occupied, unknown):
    depth, rows, columns = occupied.shape
    own = depth // lax.axis_size("robot")
    vmem = pl.BlockSpec(memory_space=pltpu.VMEM)
    smem = pl.BlockSpec(memory_space=pltpu.SMEM)
    f32 = jnp.float32

    def call(kernel, out_shape, scratch, *args, scalar=False, work=4e6):
        in_specs = [smem if scalar and n == 0 else vmem for n in range(len(args))]
        return pl.pallas_call(
            kernel,
            out_shape=out_shape,
            in_specs=in_specs,
            out_specs=jax.tree.map(lambda _: vmem, out_shape),
            scratch_shapes=scratch,
            compiler_params=pltpu.CompilerParams(vmem_limit_bytes=16 * 2**20),
            cost_estimate=pl.CostEstimate(flops=int(work), bytes_accessed=2**20, transcendentals=0),
        )(*args)

    place = jnp.stack([lax.axis_index("robot"), lax.axis_index("yz")]).astype(jnp.int32)
    lowest = jnp.min(seed_cost, axis=0)
    other = lax.ppermute(lowest, "robot", [(0, 1), (1, 0)])
    raised = call(
        prepare_kernel, jax.ShapeDtypeStruct((FIELDS, depth, rows, columns), f32), [], occupied, unknown
    )
    planes = call(
        depth_kernel,
        jax.ShapeDtypeStruct((own, FIELDS, rows, columns), jnp.int16),
        [pltpu.VMEM((FIELDS, depth, rows, columns), f32), pltpu.VMEM((FIELDS, own, rows, columns), f32)],
        place,
        lowest,
        other,
        raised,
        scalar=True,
    )
    crossed = lax.all_to_all(planes, "xy", split_axis=0, concat_axis=0, tiled=True)

    parts = lax.axis_size("yz")
    share = LINE // parts
    scratch = [
        pltpu.VMEM((LINE, LANES), f32),
        pltpu.VMEM((LINE, LANES), f32),
        pltpu.VMEM((2 * LINE, LANES), f32),
        pltpu.SMEM((BLOCKS,), jnp.int32),
    ]
    shapes = (jax.ShapeDtypeStruct((columns, share), f32),)
    shapes += (jax.ShapeDtypeStruct((columns, share), jnp.int16),) * (parts - 1)
    settled = []
    for field in range(FIELDS):
        own_part, *others = call(
            functools.partial(row_kernel, field), shapes, scratch, place, crossed, scalar=True
        )
        got = [
            lax.ppermute(part, "yz", [(i, i ^ step) for i in range(parts)])
            for step, part in enumerate(others, 1)
        ]
        settled.append((own_part, *got))
    outside = call(
        column_kernel, jax.ShapeDtypeStruct((LINE, share), f32), scratch[1:], place, *settled[0], scalar=True
    )
    signed = call(
        last_kernel, jax.ShapeDtypeStruct((share, LINE), f32), scratch, place, outside, *settled[1], scalar=True
    )
    return signed[None]


def solution(mesh):
    in_specs = (P("robot", None, "xy", "yz"), P(None, "xy", "yz"), P(None, "xy", "yz"))
    out_specs = P(("robot", "xy"), "yz", None)
    return jax.shard_map(body, mesh=mesh, in_specs=in_specs, out_specs=out_specs, check_vma=False)
```

```python
import functools

import jax
import jax.numpy as jnp
from jax import lax
from jax.experimental import pallas as pl
from jax.experimental.pallas import tpu as pltpu
from jax.sharding import PartitionSpec as P

penalty = 1048576.0
voxel_size = 0.2

LANES = 128
ROWS = 8
LINE = 512
BLOCK = 32
BLOCKS = LINE // BLOCK
GROUPS = BLOCK // ROWS
PAD = ROWS
FIELDS = 2

STEPS = 65520.0 / 13.8629653
HALF_RANGE = 32768


def encode(value):
    code = (jnp.log(1.0 + value) * STEPS + 0.5).astype(jnp.int32)
    return (code - HALF_RANGE).astype(jnp.int16)


def decode(code):
    scaled = (code.astype(jnp.int32) + HALF_RANGE).astype(jnp.float32) * (1.0 / STEPS)
    return jnp.maximum(jnp.exp(scaled) - 1.0, 0.0)


def prepare_kernel(occupied_ref, unknown_ref, raise_ref):
    def masks(place, _):
        taken = occupied_ref[place] == 1
        hidden = taken | (unknown_ref[place] == 1)
        raise_ref[0, place] = jnp.where(taken, 0.0, penalty)
        raise_ref[1, place] = jnp.where(hidden, penalty, 0.0)
        return 0

    lax.fori_loop(0, occupied_ref.shape[0], masks, 0, unroll=4)


def depth_kernel(place_ref, mine_ref, other_ref, raise_ref, out_ref, field_ref, best_ref):
    half = place_ref[0]
    depth = mine_ref.shape[0]
    own = out_ref.shape[0]

    def seed(place, _):
        source = place + half * (depth - 1 - 2 * place)
        merged = jnp.minimum(mine_ref[source], other_ref[source]).astype(jnp.float32)
        for field in range(FIELDS):
            field_ref[field, place] = merged + raise_ref[field, source]
        return 0

    lax.fori_loop(0, depth, seed, 0, unroll=4)
    groups = field_ref.shape[2] // ROWS

    def sweep(piece, _):
        field = piece // groups
        rows = pl.ds(pl.multiple_of((piece - field * groups) * ROWS, ROWS), ROWS)
        best = [None] * own
        for source in range(depth):
            value = field_ref[field, source, rows, :]
            for target in range(own):
                candidate = value + float((target - source) ** 2)
                best[target] = candidate if best[target] is None else jnp.minimum(best[target], candidate)
        for target in range(own):
            best_ref[field, target, rows, :] = best[target]
        return 0

    lax.fori_loop(0, FIELDS * groups, sweep, 0)

    def send(target, _):
        place = target + half * (own - 1 - 2 * target)
        for field in range(FIELDS):
            out_ref[place, field] = encode(best_ref[field, target])
        return 0

    lax.fori_loop(0, own, send, 0, unroll=4)


def find_blocks(line_ref, kept_ref, least_gap=0.0, reached_ref=None):
    sublane = lax.broadcasted_iota(jnp.int32, (ROWS, LANES), 0).astype(jnp.float32)
    low = []
    for block in range(BLOCKS):
        at = PAD + block * BLOCK
        least = line_ref[at : at + ROWS, :]
        for group in range(1, GROUPS):
            least = jnp.minimum(least, line_ref[at + group * ROWS : at + (group + 1) * ROWS, :])
        low.append(jnp.broadcast_to(jnp.min(least, axis=0, keepdims=True), (ROWS, LANES)))
    some = jnp.int32(0)
    for first in range(0, BLOCKS, ROWS):
        bound = jnp.full((ROWS, LANES), penalty, jnp.float32)
        if reached_ref is not None:
            bound = jnp.minimum(bound, reached_ref[first : first + ROWS, :])
        floor = []
        for block in range(BLOCKS):
            away = jnp.abs(sublane + float(first - block)) * float(BLOCK)
            far = away + float(BLOCK - 1)
            near = jnp.maximum(away - float(BLOCK - 1), least_gap)
            bound = jnp.minimum(bound, low[block] + far * far)
            floor.append(low[block] + near * near)
        kept = jnp.zeros((ROWS, 1), jnp.int32)
        for block in range(BLOCKS):
            keep = jnp.min(floor[block] - bound, axis=1, keepdims=True) < 0.0
            kept = kept | jnp.where(keep, 1 << block, 0)
        for row in range(ROWS):
            word = kept[row, 0]
            kept_ref[first + row] = word
            some = some | jnp.where(word != 0, jnp.int32(1 << (first + row)), 0)
    return some


def lower_block(line_ref, far_ref, table_ref, kept_ref, block, start):
    def left(carry):
        return carry[0] != 0

    def pair(carry):
        kept, source, best = carry
        base = pl.multiple_of((block - source) * BLOCK + LINE, BLOCK)
        row = pl.multiple_of(source * BLOCK, BLOCK) + PAD
        kept = kept ^ lax.shift_left(jnp.int32(1), source)
        best = list(best)
        for p in range(ROWS):
            squares = {k: table_ref[pl.ds(base + (k * ROWS - p), ROWS), :] for k in range(1 - GROUPS, GROUPS)}
            for q in range(GROUPS):
                value = jnp.broadcast_to(line_ref[pl.ds(row + q * ROWS + p, 1), :], (ROWS, LANES))
                for group in range(GROUPS):
                    best[group] = jnp.minimum(best[group], value + squares[group - q])
        return kept, 31 - lax.clz(kept), tuple(best)

    kept = kept_ref[block]
    best = lax.while_loop(left, pair, (kept, 31 - lax.clz(kept), start))[2]
    at = pl.multiple_of(block * BLOCK, BLOCK)
    for group in range(GROUPS):
        far_ref[pl.ds(at + group * ROWS, ROWS), :] = best[group]


def fill_table(table_ref):
    sublane = lax.broadcasted_iota(jnp.int32, (ROWS, LANES), 0).astype(jnp.float32)
    for at in range(0, 2 * LINE, ROWS):
        apart = sublane + float(at - LINE)
        table_ref[at : at + ROWS, :] = apart * apart


def sparse_pass(line_ref, far_ref, table_ref, kept_ref, _):
    fill_table(table_ref)
    find_blocks(line_ref, kept_ref)

    def target(block, _):
        at = pl.multiple_of(block * BLOCK, BLOCK) + PAD
        start = tuple(line_ref[pl.ds(at + group * ROWS, ROWS), :] for group in range(GROUPS))
        lower_block(line_ref, far_ref, table_ref, kept_ref, block, start)
        return 0

    lax.fori_loop(0, BLOCKS, target, 0)


def dense_pass(line_ref, far_ref, table_ref, kept_ref, reached_ref):
    fill_table(table_ref)
    margin = jnp.full((PAD, LANES), 3e38, jnp.float32)
    line_ref[:PAD, :] = margin
    line_ref[PAD + LINE :, :] = margin

    def band(block, _):
        at = pl.multiple_of(block * BLOCK, BLOCK)
        best = [None] * GROUPS
        for p in range(ROWS):
            first = LINE - p
            squares = {k: table_ref[first + k * ROWS : first + (k + 1) * ROWS, :] for k in (-1, 0, 1)}
            for q in range(-1, GROUPS + 1):
                value = jnp.broadcast_to(line_ref[pl.ds(at + (PAD + q * ROWS + p), 1), :], (ROWS, LANES))
                for group in range(max(q - 1, 0), min(q + 2, GROUPS)):
                    candidate = value + squares[group - q]
                    best[group] = candidate if best[group] is None else jnp.minimum(best[group], candidate)
        most = best[0]
        for group in range(GROUPS):
            far_ref[pl.ds(at + group * ROWS, ROWS), :] = best[group]
            most = jnp.maximum(most, best[group])
        reached_ref[pl.ds(block, 1), :] = jnp.max(most, axis=0, keepdims=True)
        return 0

    lax.fori_loop(0, BLOCKS, band, 0, unroll=2)

    def left(some):
        return some != 0

    def target(some):
        block = 31 - lax.clz(some)
        at = pl.multiple_of(block * BLOCK, BLOCK)
        start = tuple(far_ref[pl.ds(at + group * ROWS, ROWS), :] for group in range(GROUPS))
        lower_block(line_ref, far_ref, table_ref, kept_ref, block, start)
        return some ^ lax.shift_left(jnp.int32(1), block)

    lax.while_loop(left, target, find_blocks(line_ref, kept_ref, float(ROWS + 1), reached_ref))


PASSES = (sparse_pass, dense_pass)


def row_kernel(field, place_ref, in_ref, own_ref, *rest):
    send_refs, (line_ref, far_ref, *scratch) = rest[:-5], rest[-5:]
    chunk = in_ref.shape[2]
    for piece in range(in_ref.shape[0]):
        line_ref[PAD + piece * chunk : PAD + (piece + 1) * chunk, :] = decode(in_ref[piece, field])
    PASSES[field](line_ref, far_ref, *scratch)
    for step in range(len(send_refs) + 1):
        part = pl.ds(pl.multiple_of((place_ref[1] ^ step) * LANES, LANES), LANES)
        value = far_ref[part, :].T
        if step:
            send_refs[step - 1][...] = encode(value)
        else:
            own_ref[...] = value


def gather_lines(place_ref, own_ref, got_refs, line_ref):
    for step in range(len(got_refs) + 1):
        part = pl.ds(pl.multiple_of((place_ref[1] ^ step) * LANES, LANES) + PAD, LANES)
        line_ref[part, :] = decode(got_refs[step - 1][...]) if step else own_ref[...]


def column_kernel(place_ref, own_ref, *rest):
    got_refs, (far_ref, line_ref, *scratch) = rest[:-5], rest[-5:]
    gather_lines(place_ref, own_ref, got_refs, line_ref)
    PASSES[0](line_ref, far_ref, *scratch)


def last_kernel(place_ref, outside_ref, own_ref, *rest):
    got_refs, (out_ref, line_ref, far_ref, *scratch) = rest[:-6], rest[-6:]
    gather_lines(place_ref, own_ref, got_refs, line_ref)
    PASSES[1](line_ref, far_ref, *scratch)
    for piece in range(LINE // LANES):
        part = pl.ds(piece * LANES, LANES)
        signed = voxel_size * (jnp.sqrt(outside_ref[part, :]) - jnp.sqrt(far_ref[part, :]))
        out_ref[:, part] = signed.T


def body(seed_cost, occupied, unknown):
    depth, rows, columns = occupied.shape
    own = depth // lax.axis_size("robot")
    vmem = pl.BlockSpec(memory_space=pltpu.VMEM)
    smem = pl.BlockSpec(memory_space=pltpu.SMEM)
    f32 = jnp.float32

    def call(kernel, out_shape, scratch, *args, scalar=False, work=4e6):
        in_specs = [smem if scalar and n == 0 else vmem for n in range(len(args))]
        return pl.pallas_call(
            kernel,
            out_shape=out_shape,
            in_specs=in_specs,
            out_specs=jax.tree.map(lambda _: vmem, out_shape),
            scratch_shapes=scratch,
            compiler_params=pltpu.CompilerParams(vmem_limit_bytes=16 * 2**20),
            cost_estimate=pl.CostEstimate(flops=int(work), bytes_accessed=2**20, transcendentals=0),
        )(*args)

    place = jnp.stack([lax.axis_index("robot"), lax.axis_index("yz")]).astype(jnp.int32)
    lowest = jnp.min(seed_cost, axis=0)
    other = lax.ppermute(lowest, "robot", [(0, 1), (1, 0)])
    raised = call(
        prepare_kernel, jax.ShapeDtypeStruct((FIELDS, depth, rows, columns), f32), [], occupied, unknown
    )
    planes = call(
        depth_kernel,
        jax.ShapeDtypeStruct((own, FIELDS, rows, columns), jnp.int16),
        [pltpu.VMEM((FIELDS, depth, rows, columns), f32), pltpu.VMEM((FIELDS, own, rows, columns), f32)],
        place,
        lowest,
        other,
        raised,
        scalar=True,
    )
    crossed = lax.all_to_all(planes, "xy", split_axis=0, concat_axis=0, tiled=True)

    parts = lax.axis_size("yz")
    share = LINE // parts
    line = pltpu.VMEM((LINE + 2 * PAD, LANES), f32)
    scratch = [
        pltpu.VMEM((2 * LINE, LANES), f32),
        pltpu.SMEM((BLOCKS,), jnp.int32),
        pltpu.VMEM((BLOCKS, LANES), f32),
    ]
    lines = [line, pltpu.VMEM((LINE, LANES), f32), *scratch]
    shapes = (jax.ShapeDtypeStruct((columns, share), f32),)
    shapes += (jax.ShapeDtypeStruct((columns, share), jnp.int16),) * (parts - 1)
    settled = []
    for field in range(FIELDS):
        own_part, *others = call(
            functools.partial(row_kernel, field), shapes, lines, place, crossed, scalar=True
        )
        got = [
            lax.ppermute(part, "yz", [(i, i ^ step) for i in range(parts)])
            for step, part in enumerate(others, 1)
        ]
        settled.append((own_part, *got))
    outside = call(
        column_kernel, jax.ShapeDtypeStruct((LINE, share), f32), [line, *scratch], place, *settled[0], scalar=True
    )
    signed = call(
        last_kernel, jax.ShapeDtypeStruct((share, LINE), f32), lines, place, outside, *settled[1], scalar=True
    )
    return signed[None]


def solution(mesh):
    in_specs = (P("robot", None, "xy", "yz"), P(None, "xy", "yz"), P(None, "xy", "yz"))
    out_specs = P(("robot", "xy"), "yz", None)
    return jax.shard_map(body, mesh=mesh, in_specs=in_specs, out_specs=out_specs, check_vma=False)
```

```python
import jax
import jax.numpy as jnp
from jax import lax
from jax.experimental import pallas as pl
from jax.experimental.pallas import tpu as pltpu
from jax.sharding import PartitionSpec as P

penalty = 1048576.0
voxel_size = 0.2

LANES = 128
ROWS = 8
LINE = 512
BLOCK = 32
BLOCKS = LINE // BLOCK
GROUPS = BLOCK // ROWS
PAD = ROWS
FIELDS = 2

STEPS = 65520.0 / 13.8629653
HALF_RANGE = 32768


def encode(value):
    code = (jnp.log(1.0 + value) * STEPS + 0.5).astype(jnp.int32)
    return (code - HALF_RANGE).astype(jnp.int16)


def decode(code):
    scaled = (code.astype(jnp.int32) + HALF_RANGE).astype(jnp.float32) * (1.0 / STEPS)
    return jnp.maximum(jnp.exp(scaled) - 1.0, 0.0)


def prepare_kernel(occupied_ref, unknown_ref, raise_ref):
    def masks(place, _):
        taken = occupied_ref[place] == 1
        hidden = taken | (unknown_ref[place] == 1)
        raise_ref[0, place] = jnp.where(taken, 0.0, penalty)
        raise_ref[1, place] = jnp.where(hidden, penalty, 0.0)
        return 0

    lax.fori_loop(0, occupied_ref.shape[0], masks, 0, unroll=4)


def depth_kernel(place_ref, mine_ref, other_ref, raise_ref, out_ref, field_ref, best_ref):
    half = place_ref[0]
    depth = mine_ref.shape[0]
    own = out_ref.shape[0]

    def seed(place, _):
        source = place + half * (depth - 1 - 2 * place)
        merged = jnp.minimum(mine_ref[source], other_ref[source]).astype(jnp.float32)
        for field in range(FIELDS):
            field_ref[field, place] = merged + raise_ref[field, source]
        return 0

    lax.fori_loop(0, depth, seed, 0, unroll=4)
    groups = field_ref.shape[2] // ROWS

    def sweep(piece, _):
        field = piece // groups
        rows = pl.ds(pl.multiple_of((piece - field * groups) * ROWS, ROWS), ROWS)
        best = [None] * own
        for source in range(depth):
            value = field_ref[field, source, rows, :]
            for target in range(own):
                candidate = value + float((target - source) ** 2)
                best[target] = candidate if best[target] is None else jnp.minimum(best[target], candidate)
        for target in range(own):
            best_ref[field, target, rows, :] = best[target]
        return 0

    lax.fori_loop(0, FIELDS * groups, sweep, 0)

    def send(target, _):
        place = target + half * (own - 1 - 2 * target)
        for field in range(FIELDS):
            out_ref[place, field] = encode(best_ref[field, target])
        return 0

    lax.fori_loop(0, own, send, 0, unroll=4)


def bit(place):
    return jnp.int32((1 << place) - (1 << 32 if place == 31 else 0))


def find_blocks(line_ref, kept_ref, size, least_gap=0.0, reached_ref=None):
    sublane = lax.broadcasted_iota(jnp.int32, (ROWS, LANES), 0).astype(jnp.float32)
    sources = range(0, LINE, size)
    low = []
    for source in sources:
        least = line_ref[PAD + source : PAD + source + ROWS, :]
        for at in range(PAD + source + ROWS, PAD + source + size, ROWS):
            least = jnp.minimum(least, line_ref[at : at + ROWS, :])
        low.append(jnp.broadcast_to(jnp.min(least, axis=0, keepdims=True), (ROWS, LANES)))
    some = jnp.int32(0)
    for first in range(0, BLOCKS, ROWS):
        bound = jnp.full((ROWS, LANES), penalty, jnp.float32)
        if reached_ref is not None:
            bound = jnp.minimum(bound, reached_ref[first : first + ROWS, :])
        floor = []
        for source, least in zip(sources, low):
            after = sublane * float(BLOCK) + float(first * BLOCK - source)
            far = jnp.maximum(after + float(BLOCK - 1), float(size - 1) - after)
            near = jnp.maximum(jnp.maximum(after - float(size - 1), -after - float(BLOCK - 1)), least_gap)
            bound = jnp.minimum(bound, least + far * far)
            floor.append(least + near * near)
        kept = jnp.zeros((ROWS, 1), jnp.int32)
        for place in range(len(sources)):
            keep = jnp.min(floor[place] - bound, axis=1, keepdims=True) < 0.0
            kept = kept | jnp.where(keep, bit(place), 0)
        for row in range(ROWS):
            word = kept[row, 0]
            kept_ref[first + row] = word
            some = some | jnp.where(word != 0, bit(first + row), 0)
    return some


def lower_block(line_ref, far_ref, table_ref, kept_ref, size, block, start):
    pieces = size // ROWS

    def left(carry):
        return carry[0] != 0

    def pair(carry):
        kept, source, best = carry
        base = pl.multiple_of(block * BLOCK - source * size + LINE, size)
        row = pl.multiple_of(source * size, size) + PAD
        kept = kept ^ lax.shift_left(jnp.int32(1), source)
        best = list(best)
        for p in range(ROWS):
            squares = {k: table_ref[pl.ds(base + (k * ROWS - p), ROWS), :] for k in range(1 - pieces, GROUPS)}
            for q in range(pieces):
                value = jnp.broadcast_to(line_ref[pl.ds(row + q * ROWS + p, 1), :], (ROWS, LANES))
                for group in range(GROUPS):
                    best[group] = jnp.minimum(best[group], value + squares[group - q])
        return kept, 31 - lax.clz(kept), tuple(best)

    kept = kept_ref[block]
    best = lax.while_loop(left, pair, (kept, 31 - lax.clz(kept), start))[2]
    at = pl.multiple_of(block * BLOCK, BLOCK)
    for group in range(GROUPS):
        far_ref[pl.ds(at + group * ROWS, ROWS), :] = best[group]


def fill_table(table_ref):
    sublane = lax.broadcasted_iota(jnp.int32, (ROWS, LANES), 0).astype(jnp.float32)
    for at in range(0, 2 * LINE, ROWS):
        apart = sublane + float(at - LINE)
        table_ref[at : at + ROWS, :] = apart * apart


def sparse_pass(line_ref, far_ref, table_ref, kept_ref, _):
    size = BLOCK // 2
    find_blocks(line_ref, kept_ref, size)

    def target(block, _):
        at = pl.multiple_of(block * BLOCK, BLOCK) + PAD
        start = tuple(line_ref[pl.ds(at + group * ROWS, ROWS), :] for group in range(GROUPS))
        lower_block(line_ref, far_ref, table_ref, kept_ref, size, block, start)
        return 0

    lax.fori_loop(0, BLOCKS, target, 0)


def dense_pass(line_ref, far_ref, table_ref, kept_ref, reached_ref):
    margin = jnp.full((PAD, LANES), 3e38, jnp.float32)
    line_ref[:PAD, :] = margin
    line_ref[PAD + LINE :, :] = margin

    def band(block, _):
        at = pl.multiple_of(block * BLOCK, BLOCK)
        best = [None] * GROUPS
        for p in range(ROWS):
            first = LINE - p
            squares = {k: table_ref[first + k * ROWS : first + (k + 1) * ROWS, :] for k in (-1, 0, 1)}
            for q in range(-1, GROUPS + 1):
                value = jnp.broadcast_to(line_ref[pl.ds(at + (PAD + q * ROWS + p), 1), :], (ROWS, LANES))
                for group in range(max(q - 1, 0), min(q + 2, GROUPS)):
                    candidate = value + squares[group - q]
                    best[group] = candidate if best[group] is None else jnp.minimum(best[group], candidate)
        most = best[0]
        for group in range(GROUPS):
            far_ref[pl.ds(at + group * ROWS, ROWS), :] = best[group]
            most = jnp.maximum(most, best[group])
        reached_ref[pl.ds(block, 1), :] = jnp.max(most, axis=0, keepdims=True)
        return 0

    lax.fori_loop(0, BLOCKS, band, 0, unroll=2)

    def left(some):
        return some != 0

    def target(some):
        block = 31 - lax.clz(some)
        at = pl.multiple_of(block * BLOCK, BLOCK)
        start = tuple(far_ref[pl.ds(at + group * ROWS, ROWS), :] for group in range(GROUPS))
        lower_block(line_ref, far_ref, table_ref, kept_ref, BLOCK, block, start)
        return some ^ lax.shift_left(jnp.int32(1), block)

    lax.while_loop(left, target, find_blocks(line_ref, kept_ref, BLOCK, float(ROWS + 1), reached_ref))


PASSES = (sparse_pass, dense_pass)


def row_kernel(place_ref, in_ref, own_ref, *rest):
    send_refs, (line_ref, far_ref, table_ref, *scratch) = rest[:-5], rest[-5:]
    chunk = in_ref.shape[2]
    fill_table(table_ref)
    for field in range(FIELDS):
        for piece in range(in_ref.shape[0]):
            line_ref[PAD + piece * chunk : PAD + (piece + 1) * chunk, :] = decode(in_ref[piece, field])
        PASSES[field](line_ref, far_ref, table_ref, *scratch)
        for step in range(len(send_refs) + 1):
            part = pl.ds(pl.multiple_of((place_ref[1] ^ step) * LANES, LANES), LANES)
            value = far_ref[part, :].T
            if step:
                send_refs[step - 1][field] = encode(value)
            else:
                own_ref[field] = value


def column_kernel(place_ref, own_ref, *rest):
    got_refs, (out_ref, line_ref, outside_ref, inside_ref, table_ref, *scratch) = rest[:-7], rest[-7:]
    fill_table(table_ref)
    for field, far_ref in enumerate((outside_ref, inside_ref)):
        for step in range(len(got_refs) + 1):
            part = pl.ds(pl.multiple_of((place_ref[1] ^ step) * LANES, LANES) + PAD, LANES)
            line_ref[part, :] = decode(got_refs[step - 1][field]) if step else own_ref[field]
        PASSES[field](line_ref, far_ref, table_ref, *scratch)
    for piece in range(LINE // LANES):
        part = pl.ds(piece * LANES, LANES)
        signed = voxel_size * (jnp.sqrt(outside_ref[part, :]) - jnp.sqrt(inside_ref[part, :]))
        out_ref[:, part] = signed.T


def body(seed_cost, occupied, unknown):
    depth, rows, columns = occupied.shape
    own = depth // lax.axis_size("robot")
    vmem = pl.BlockSpec(memory_space=pltpu.VMEM)
    smem = pl.BlockSpec(memory_space=pltpu.SMEM)
    f32 = jnp.float32

    def call(kernel, out_shape, scratch, *args, scalar=False, work=4e6):
        in_specs = [smem if scalar and n == 0 else vmem for n in range(len(args))]
        return pl.pallas_call(
            kernel,
            out_shape=out_shape,
            in_specs=in_specs,
            out_specs=jax.tree.map(lambda _: vmem, out_shape),
            scratch_shapes=scratch,
            compiler_params=pltpu.CompilerParams(vmem_limit_bytes=16 * 2**20),
            cost_estimate=pl.CostEstimate(flops=int(work), bytes_accessed=2**20, transcendentals=0),
        )(*args)

    place = jnp.stack([lax.axis_index("robot"), lax.axis_index("yz")]).astype(jnp.int32)
    lowest = jnp.min(seed_cost, axis=0)
    other = lax.ppermute(lowest, "robot", [(0, 1), (1, 0)])
    raised = call(
        prepare_kernel, jax.ShapeDtypeStruct((FIELDS, depth, rows, columns), f32), [], occupied, unknown
    )
    planes = call(
        depth_kernel,
        jax.ShapeDtypeStruct((own, FIELDS, rows, columns), jnp.int16),
        [pltpu.VMEM((FIELDS, depth, rows, columns), f32), pltpu.VMEM((FIELDS, own, rows, columns), f32)],
        place,
        lowest,
        other,
        raised,
        scalar=True,
    )
    crossed = lax.all_to_all(planes, "xy", split_axis=0, concat_axis=0, tiled=True)

    parts = lax.axis_size("yz")
    share = LINE // parts
    line = pltpu.VMEM((LINE + 2 * PAD, LANES), f32)
    far = pltpu.VMEM((LINE, LANES), f32)
    scratch = [
        pltpu.VMEM((2 * LINE, LANES), f32),
        pltpu.SMEM((BLOCKS,), jnp.int32),
        pltpu.VMEM((BLOCKS, LANES), f32),
    ]
    shapes = (jax.ShapeDtypeStruct((FIELDS, columns, share), f32),)
    shapes += (jax.ShapeDtypeStruct((FIELDS, columns, share), jnp.int16),) * (parts - 1)
    own_part, *others = call(row_kernel, shapes, [line, far, *scratch], place, crossed, scalar=True)
    got = [
        lax.ppermute(part, "yz", [(i, i ^ step) for i in range(parts)]) for step, part in enumerate(others, 1)
    ]
    signed = call(
        column_kernel,
        jax.ShapeDtypeStruct((share, LINE), f32),
        [line, far, far, *scratch],
        place,
        own_part,
        *got,
        scalar=True,
    )
    return signed[None]


def solution(mesh):
    in_specs = (P("robot", None, "xy", "yz"), P(None, "xy", "yz"), P(None, "xy", "yz"))
    out_specs = P(("robot", "xy"), "yz", None)
    return jax.shard_map(body, mesh=mesh, in_specs=in_specs, out_specs=out_specs, check_vma=False)
```

```python
import functools

import jax
import jax.numpy as jnp
from jax import lax
from jax.experimental import pallas as pl
from jax.experimental.pallas import tpu as pltpu
from jax.sharding import PartitionSpec as P

penalty = 1048576.0
voxel_size = 0.2

LANES = 128
ROWS = 8
LINE = 512
BLOCK = 32
BLOCKS = LINE // BLOCK
GROUPS = BLOCK // ROWS
PAD = ROWS
FIELDS = 2

STEPS = 65520.0 / 13.8629653
HALF_RANGE = 32768


def encode(value):
    code = (jnp.log(1.0 + value) * STEPS + 0.5).astype(jnp.int32)
    return (code - HALF_RANGE).astype(jnp.int16)


def decode(code):
    scaled = (code.astype(jnp.int32) + HALF_RANGE).astype(jnp.float32) * (1.0 / STEPS)
    return jnp.maximum(jnp.exp(scaled) - 1.0, 0.0)


def prepare_kernel(occupied_ref, unknown_ref, raise_ref):
    def masks(place, _):
        taken = occupied_ref[place] == 1
        hidden = taken | (unknown_ref[place] == 1)
        raise_ref[0, place] = jnp.where(taken, 0.0, penalty)
        raise_ref[1, place] = jnp.where(hidden, penalty, 0.0)
        return 0

    lax.fori_loop(0, occupied_ref.shape[0], masks, 0, unroll=4)


def depth_kernel(mine_ref, other_ref, raise_ref, out_ref, field_ref, best_ref):
    half = lax.axis_index("robot")
    depth = mine_ref.shape[0]
    own = out_ref.shape[0]

    def seed(place, _):
        source = place + half * (depth - 1 - 2 * place)
        merged = jnp.minimum(mine_ref[source], other_ref[source]).astype(jnp.float32)
        for field in range(FIELDS):
            field_ref[field, place] = merged + raise_ref[field, source]
        return 0

    lax.fori_loop(0, depth, seed, 0, unroll=4)
    groups = field_ref.shape[2] // ROWS

    def sweep(piece, _):
        field = piece // groups
        rows = pl.ds(pl.multiple_of((piece - field * groups) * ROWS, ROWS), ROWS)
        best = [None] * own
        for source in range(depth):
            value = field_ref[field, source, rows, :]
            for target in range(own):
                candidate = value + float((target - source) ** 2)
                best[target] = candidate if best[target] is None else jnp.minimum(best[target], candidate)
        for target in range(own):
            best_ref[field, target, rows, :] = best[target]
        return 0

    lax.fori_loop(0, FIELDS * groups, sweep, 0)

    def send(target, _):
        place = target + half * (own - 1 - 2 * target)
        for field in range(FIELDS):
            out_ref[place, field] = encode(best_ref[field, target])
        return 0

    lax.fori_loop(0, own, send, 0, unroll=4)


def bit(place):
    return jnp.int32((1 << place) - (1 << 32 if place == 31 else 0))


def find_blocks(line_ref, kept_ref, size, least_gap=0.0, reached_ref=None):
    sublane = lax.broadcasted_iota(jnp.int32, (ROWS, LANES), 0).astype(jnp.float32)
    sources = range(0, LINE, size)
    low = []
    for source in sources:
        least = line_ref[PAD + source : PAD + source + ROWS, :]
        for at in range(PAD + source + ROWS, PAD + source + size, ROWS):
            least = jnp.minimum(least, line_ref[at : at + ROWS, :])
        low.append(jnp.broadcast_to(jnp.min(least, axis=0, keepdims=True), (ROWS, LANES)))
    some = jnp.int32(0)
    for first in range(0, BLOCKS, ROWS):
        bound = jnp.full((ROWS, LANES), penalty, jnp.float32)
        if reached_ref is not None:
            bound = jnp.minimum(bound, reached_ref[first : first + ROWS, :])
        floor = []
        for source, least in zip(sources, low):
            after = sublane * float(BLOCK) + float(first * BLOCK - source)
            far = jnp.maximum(after + float(BLOCK - 1), float(size - 1) - after)
            near = jnp.maximum(jnp.maximum(after - float(size - 1), -after - float(BLOCK - 1)), least_gap)
            bound = jnp.minimum(bound, least + far * far)
            floor.append(least + near * near)
        kept = jnp.zeros((ROWS, 1), jnp.int32)
        for place in range(len(sources)):
            keep = jnp.min(floor[place] - bound, axis=1, keepdims=True) < 0.0
            kept = kept | jnp.where(keep, bit(place), 0)
        for row in range(ROWS):
            word = kept[row, 0]
            kept_ref[first + row] = word
            some = some | jnp.where(word != 0, bit(first + row), 0)
    return some


def lower_block(line_ref, far_ref, table_ref, kept_ref, size, block, start):
    pieces = size // ROWS

    def left(carry):
        return carry[0] != 0

    def pair(carry):
        kept, source, best = carry
        base = pl.multiple_of(block * BLOCK - source * size + LINE, size)
        row = pl.multiple_of(source * size, size) + PAD
        kept = kept ^ lax.shift_left(jnp.int32(1), source)
        best = list(best)
        for p in range(ROWS):
            squares = {k: table_ref[pl.ds(base + (k * ROWS - p), ROWS), :] for k in range(1 - pieces, GROUPS)}
            for q in range(pieces):
                value = jnp.broadcast_to(line_ref[pl.ds(row + q * ROWS + p, 1), :], (ROWS, LANES))
                for group in range(GROUPS):
                    best[group] = jnp.minimum(best[group], value + squares[group - q])
        return kept, 31 - lax.clz(kept), tuple(best)

    kept = kept_ref[block]
    best = lax.while_loop(left, pair, (kept, 31 - lax.clz(kept), start))[2]
    at = pl.multiple_of(block * BLOCK, BLOCK)
    for group in range(GROUPS):
        far_ref[pl.ds(at + group * ROWS, ROWS), :] = best[group]


def fill_table(table_ref):
    sublane = lax.broadcasted_iota(jnp.int32, (ROWS, LANES), 0).astype(jnp.float32)
    for at in range(0, 2 * LINE, ROWS):
        apart = sublane + float(at - LINE)
        table_ref[at : at + ROWS, :] = apart * apart


def sparse_pass(line_ref, far_ref, table_ref, kept_ref, _):
    size = BLOCK // 2
    fill_table(table_ref)
    find_blocks(line_ref, kept_ref, size)

    def target(block, _):
        at = pl.multiple_of(block * BLOCK, BLOCK) + PAD
        start = tuple(line_ref[pl.ds(at + group * ROWS, ROWS), :] for group in range(GROUPS))
        lower_block(line_ref, far_ref, table_ref, kept_ref, size, block, start)
        return 0

    lax.fori_loop(0, BLOCKS, target, 0)


def dense_pass(line_ref, far_ref, table_ref, kept_ref, reached_ref):
    fill_table(table_ref)
    margin = jnp.full((PAD, LANES), 3e38, jnp.float32)
    line_ref[:PAD, :] = margin
    line_ref[PAD + LINE :, :] = margin

    def band(block, _):
        at = pl.multiple_of(block * BLOCK, BLOCK)
        best = [None] * GROUPS
        for p in range(ROWS):
            first = LINE - p
            squares = {k: table_ref[first + k * ROWS : first + (k + 1) * ROWS, :] for k in (-1, 0, 1)}
            for q in range(-1, GROUPS + 1):
                value = jnp.broadcast_to(line_ref[pl.ds(at + (PAD + q * ROWS + p), 1), :], (ROWS, LANES))
                for group in range(max(q - 1, 0), min(q + 2, GROUPS)):
                    candidate = value + squares[group - q]
                    best[group] = candidate if best[group] is None else jnp.minimum(best[group], candidate)
        most = best[0]
        for group in range(GROUPS):
            far_ref[pl.ds(at + group * ROWS, ROWS), :] = best[group]
            most = jnp.maximum(most, best[group])
        reached_ref[pl.ds(block, 1), :] = jnp.max(most, axis=0, keepdims=True)
        return 0

    lax.fori_loop(0, BLOCKS, band, 0, unroll=2)

    def left(some):
        return some != 0

    def target(some):
        block = 31 - lax.clz(some)
        at = pl.multiple_of(block * BLOCK, BLOCK)
        start = tuple(far_ref[pl.ds(at + group * ROWS, ROWS), :] for group in range(GROUPS))
        lower_block(line_ref, far_ref, table_ref, kept_ref, BLOCK, block, start)
        return some ^ lax.shift_left(jnp.int32(1), block)

    lax.while_loop(left, target, find_blocks(line_ref, kept_ref, BLOCK, float(ROWS + 1), reached_ref))


PASSES = (sparse_pass, dense_pass)


def row_kernel(field, in_ref, own_ref, *rest):
    send_refs, (line_ref, far_ref, *scratch) = rest[:-5], rest[-5:]
    chunk = in_ref.shape[2]
    for piece in range(in_ref.shape[0]):
        line_ref[PAD + piece * chunk : PAD + (piece + 1) * chunk, :] = decode(in_ref[piece, field])
    PASSES[field](line_ref, far_ref, *scratch)
    for step in range(len(send_refs) + 1):
        part = pl.ds(pl.multiple_of((lax.axis_index("yz") ^ step) * LANES, LANES), LANES)
        value = far_ref[part, :].T
        if step:
            send_refs[step - 1][...] = encode(value)
        else:
            own_ref[...] = value


def gather_lines(own_ref, got_refs, line_ref):
    for step in range(len(got_refs) + 1):
        part = pl.ds(pl.multiple_of((lax.axis_index("yz") ^ step) * LANES, LANES) + PAD, LANES)
        line_ref[part, :] = decode(got_refs[step - 1][...]) if step else own_ref[...]


def column_kernel(own_ref, *rest):
    got_refs, (far_ref, line_ref, *scratch) = rest[:-5], rest[-5:]
    gather_lines(own_ref, got_refs, line_ref)
    PASSES[0](line_ref, far_ref, *scratch)


def last_kernel(outside_ref, own_ref, *rest):
    got_refs, (out_ref, line_ref, far_ref, *scratch) = rest[:-6], rest[-6:]
    gather_lines(own_ref, got_refs, line_ref)
    PASSES[1](line_ref, far_ref, *scratch)
    for piece in range(LINE // LANES):
        part = pl.ds(piece * LANES, LANES)
        signed = voxel_size * (jnp.sqrt(outside_ref[part, :]) - jnp.sqrt(far_ref[part, :]))
        out_ref[:, part] = signed.T


def body(seed_cost, occupied, unknown):
    depth, rows, columns = occupied.shape
    own = depth // lax.axis_size("robot")
    vmem = pl.BlockSpec(memory_space=pltpu.VMEM)
    f32 = jnp.float32

    def call(kernel, out_shape, scratch, *args, work=4e6):
        return pl.pallas_call(
            kernel,
            out_shape=out_shape,
            in_specs=[vmem] * len(args),
            out_specs=jax.tree.map(lambda _: vmem, out_shape),
            scratch_shapes=scratch,
            compiler_params=pltpu.CompilerParams(vmem_limit_bytes=16 * 2**20),
            cost_estimate=pl.CostEstimate(flops=int(work), bytes_accessed=2**20, transcendentals=0),
        )(*args)

    lowest = jnp.min(seed_cost, axis=0)
    other = lax.ppermute(lowest, "robot", [(0, 1), (1, 0)])
    raised = call(
        prepare_kernel, jax.ShapeDtypeStruct((FIELDS, depth, rows, columns), f32), [], occupied, unknown
    )
    planes = call(
        depth_kernel,
        jax.ShapeDtypeStruct((own, FIELDS, rows, columns), jnp.int16),
        [pltpu.VMEM((FIELDS, depth, rows, columns), f32), pltpu.VMEM((FIELDS, own, rows, columns), f32)],
        lowest,
        other,
        raised,
    )
    crossed = lax.all_to_all(planes, "xy", split_axis=0, concat_axis=0, tiled=True)

    parts = lax.axis_size("yz")
    share = LINE // parts
    line = pltpu.VMEM((LINE + 2 * PAD, LANES), f32)
    scratch = [
        pltpu.VMEM((2 * LINE, LANES), f32),
        pltpu.SMEM((BLOCKS,), jnp.int32),
        pltpu.VMEM((BLOCKS, LANES), f32),
    ]
    lines = [line, pltpu.VMEM((LINE, LANES), f32), *scratch]
    shapes = (jax.ShapeDtypeStruct((columns, share), f32),)
    shapes += (jax.ShapeDtypeStruct((columns, share), jnp.int16),) * (parts - 1)
    settled = []
    for field in range(FIELDS):
        own_part, *others = call(
            functools.partial(row_kernel, field), shapes, lines, crossed
        )
        got = [
            lax.ppermute(part, "yz", [(i, i ^ step) for i in range(parts)])
            for step, part in enumerate(others, 1)
        ]
        settled.append((own_part, *got))
    outside = call(
        column_kernel, jax.ShapeDtypeStruct((LINE, share), f32), [line, *scratch], *settled[0]
    )
    signed = call(
        last_kernel, jax.ShapeDtypeStruct((share, LINE), f32), lines, outside, *settled[1]
    )
    return signed[None]


def solution(mesh):
    in_specs = (P("robot", None, "xy", "yz"), P(None, "xy", "yz"), P(None, "xy", "yz"))
    out_specs = P(("robot", "xy"), "yz", None)
    return jax.shard_map(body, mesh=mesh, in_specs=in_specs, out_specs=out_specs, check_vma=False)
```

```python
import functools

import jax
import jax.numpy as jnp
from jax import lax
from jax.experimental import pallas as pl
from jax.experimental.pallas import tpu as pltpu
from jax.sharding import PartitionSpec as P

penalty = 1048576.0
voxel_size = 0.2

LANES = 128
ROWS = 8
LINE = 512
BLOCK = 32
BLOCKS = LINE // BLOCK
GROUPS = BLOCK // ROWS
PAD = ROWS
FIELDS = 2

STEPS = 65520.0 / 13.8629653
HALF_RANGE = 32768


def encode(value):
    code = (jnp.log(1.0 + value) * STEPS + 0.5).astype(jnp.int32)
    return (code - HALF_RANGE).astype(jnp.int16)


def decode(code):
    scaled = (code.astype(jnp.int32) + HALF_RANGE).astype(jnp.float32) * (1.0 / STEPS)
    return jnp.maximum(jnp.exp(scaled) - 1.0, 0.0)


def lowest_kernel(cost_ref, out_ref, buffer_ref, least_ref, in_sems, out_sems):
    parts = in_sems.shape[0]
    step = out_ref.shape[0] // parts
    arrive, leave = [], []
    for part in range(parts):
        planes = pl.ds(part * step, step)
        arrive.append(pltpu.make_async_copy(cost_ref.at[:, planes], buffer_ref.at[:, planes], in_sems.at[part]))
        leave.append(pltpu.make_async_copy(least_ref.at[planes], out_ref.at[planes], out_sems.at[part]))
    for copy in arrive:
        copy.start()
    for part in range(parts):
        arrive[part].wait()
        planes = pl.ds(part * step, step)
        least = buffer_ref[0, planes]
        for robot in range(1, buffer_ref.shape[0]):
            least = jnp.minimum(least, buffer_ref[robot, planes])
        least_ref[planes] = least
        leave[part].start()
    for copy in leave:
        copy.wait()


def prepare_kernel(occupied_ref, unknown_ref, raise_ref):
    def masks(place, _):
        taken = occupied_ref[place] == 1
        hidden = taken | (unknown_ref[place] == 1)
        raise_ref[0, place] = jnp.where(taken, 0.0, penalty)
        raise_ref[1, place] = jnp.where(hidden, penalty, 0.0)
        return 0

    lax.fori_loop(0, occupied_ref.shape[0], masks, 0, unroll=4)


def depth_kernel(mine_ref, other_ref, raise_ref, out_ref, field_ref, best_ref):
    half = lax.axis_index("robot")
    depth = mine_ref.shape[0]
    own = out_ref.shape[0]

    def seed(place, _):
        source = place + half * (depth - 1 - 2 * place)
        merged = jnp.minimum(mine_ref[source], other_ref[source]).astype(jnp.float32)
        for field in range(FIELDS):
            field_ref[field, place] = merged + raise_ref[field, source]
        return 0

    lax.fori_loop(0, depth, seed, 0, unroll=8)
    groups = field_ref.shape[2] // ROWS

    def sweep(piece, _):
        field = piece // groups
        rows = pl.ds(pl.multiple_of((piece - field * groups) * ROWS, ROWS), ROWS)
        best = [None] * own
        for source in range(depth):
            value = field_ref[field, source, rows, :]
            for target in range(own):
                candidate = value + float((target - source) ** 2)
                best[target] = candidate if best[target] is None else jnp.minimum(best[target], candidate)
        for target in range(own):
            best_ref[field, target, rows, :] = best[target]
        return 0

    lax.fori_loop(0, FIELDS * groups, sweep, 0)

    def send(target, _):
        place = target + half * (own - 1 - 2 * target)
        for field in range(FIELDS):
            out_ref[place, field] = encode(best_ref[field, target])
        return 0

    lax.fori_loop(0, own, send, 0, unroll=8)


def bit(place):
    return jnp.int32((1 << place) - (1 << 32 if place == 31 else 0))


def find_blocks(line_ref, kept_ref, size, least_gap=0.0, reached_ref=None):
    sublane = lax.broadcasted_iota(jnp.int32, (ROWS, LANES), 0).astype(jnp.float32)
    sources = range(0, LINE, size)
    low = []
    for source in sources:
        least = line_ref[PAD + source : PAD + source + ROWS, :]
        for at in range(PAD + source + ROWS, PAD + source + size, ROWS):
            least = jnp.minimum(least, line_ref[at : at + ROWS, :])
        low.append(jnp.broadcast_to(jnp.min(least, axis=0, keepdims=True), (ROWS, LANES)))
    some = jnp.int32(0)
    for first in range(0, BLOCKS, ROWS):
        bound = jnp.full((ROWS, LANES), penalty, jnp.float32)
        if reached_ref is not None:
            bound = jnp.minimum(bound, reached_ref[first : first + ROWS, :])
        floor = []
        for source, least in zip(sources, low):
            after = sublane * float(BLOCK) + float(first * BLOCK - source)
            far = jnp.maximum(after + float(BLOCK - 1), float(size - 1) - after)
            near = jnp.maximum(jnp.maximum(after - float(size - 1), -after - float(BLOCK - 1)), least_gap)
            bound = jnp.minimum(bound, least + far * far)
            floor.append(least + near * near)
        kept = jnp.zeros((ROWS, 1), jnp.int32)
        for place in range(len(sources)):
            keep = jnp.min(floor[place] - bound, axis=1, keepdims=True) < 0.0
            kept = kept | jnp.where(keep, bit(place), 0)
        for row in range(ROWS):
            word = kept[row, 0]
            kept_ref[first + row] = word
            some = some | jnp.where(word != 0, bit(first + row), 0)
    return some


def lower_block(line_ref, far_ref, table_ref, kept_ref, size, block, start):
    pieces = size // ROWS

    def left(carry):
        return carry[0] != 0

    def pair(carry):
        kept, source, best = carry
        base = pl.multiple_of(block * BLOCK - source * size + LINE, size)
        row = pl.multiple_of(source * size, size) + PAD
        kept = kept ^ lax.shift_left(jnp.int32(1), source)
        best = list(best)
        for p in range(ROWS):
            squares = {k: table_ref[pl.ds(base + (k * ROWS - p), ROWS), :] for k in range(1 - pieces, GROUPS)}
            for q in range(pieces):
                value = jnp.broadcast_to(line_ref[pl.ds(row + q * ROWS + p, 1), :], (ROWS, LANES))
                for group in range(GROUPS):
                    best[group] = jnp.minimum(best[group], value + squares[group - q])
        return kept, 31 - lax.clz(kept), tuple(best)

    kept = kept_ref[block]
    best = lax.while_loop(left, pair, (kept, 31 - lax.clz(kept), start))[2]
    at = pl.multiple_of(block * BLOCK, BLOCK)
    for group in range(GROUPS):
        far_ref[pl.ds(at + group * ROWS, ROWS), :] = best[group]


def fill_table(table_ref):
    sublane = lax.broadcasted_iota(jnp.int32, (ROWS, LANES), 0).astype(jnp.float32)
    for at in range(0, 2 * LINE, ROWS):
        apart = sublane + float(at - LINE)
        table_ref[at : at + ROWS, :] = apart * apart


def sparse_pass(line_ref, far_ref, table_ref, kept_ref, _):
    size = BLOCK // 2
    find_blocks(line_ref, kept_ref, size)

    def target(block, _):
        at = pl.multiple_of(block * BLOCK, BLOCK) + PAD
        start = tuple(line_ref[pl.ds(at + group * ROWS, ROWS), :] for group in range(GROUPS))
        lower_block(line_ref, far_ref, table_ref, kept_ref, size, block, start)
        return 0

    lax.fori_loop(0, BLOCKS, target, 0)


def dense_pass(line_ref, far_ref, table_ref, kept_ref, reached_ref, finish=None):
    margin = jnp.full((PAD, LANES), 3e38, jnp.float32)
    line_ref[:PAD, :] = margin
    line_ref[PAD + LINE :, :] = margin

    def band(block, _):
        at = pl.multiple_of(block * BLOCK, BLOCK)
        best = [None] * GROUPS
        for p in range(ROWS):
            first = LINE - p
            squares = {k: table_ref[first + k * ROWS : first + (k + 1) * ROWS, :] for k in (-1, 0, 1)}
            for q in range(-1, GROUPS + 1):
                value = jnp.broadcast_to(line_ref[pl.ds(at + (PAD + q * ROWS + p), 1), :], (ROWS, LANES))
                for group in range(max(q - 1, 0), min(q + 2, GROUPS)):
                    candidate = value + squares[group - q]
                    best[group] = candidate if best[group] is None else jnp.minimum(best[group], candidate)
        most = best[0]
        for group in range(GROUPS):
            far_ref[pl.ds(at + group * ROWS, ROWS), :] = best[group]
            most = jnp.maximum(most, best[group])
        reached_ref[pl.ds(block, 1), :] = jnp.max(most, axis=0, keepdims=True)
        return 0

    lax.fori_loop(0, BLOCKS, band, 0, unroll=2)

    def left(some):
        return some != 0

    def target(some):
        block = 31 - lax.clz(some)
        at = pl.multiple_of(block * BLOCK, BLOCK)
        start = tuple(far_ref[pl.ds(at + group * ROWS, ROWS), :] for group in range(GROUPS))
        lower_block(line_ref, far_ref, table_ref, kept_ref, BLOCK, block, start)
        return some ^ lax.shift_left(jnp.int32(1), block)

    some = find_blocks(line_ref, kept_ref, BLOCK, float(ROWS + 1), reached_ref)
    if finish is None:
        lax.while_loop(left, target, some)
        return
    per_part = LANES // BLOCK
    for part in range(LINE // LANES):
        lax.while_loop(left, target, some & (((1 << per_part) - 1) << (part * per_part)))
        finish(part)


PASSES = (sparse_pass, dense_pass)


def row_kernel(field, in_ref, table_ref, own_ref, *rest):
    send_refs, (line_ref, far_ref, *scratch) = rest[:-4], rest[-4:]
    chunk = in_ref.shape[2]
    if field == 0:
        fill_table(table_ref)
    for piece in range(in_ref.shape[0]):
        line_ref[PAD + piece * chunk : PAD + (piece + 1) * chunk, :] = decode(in_ref[piece, field])
    PASSES[field](line_ref, far_ref, table_ref, *scratch)
    for step in range(len(send_refs) + 1):
        part = pl.ds(pl.multiple_of((lax.axis_index("yz") ^ step) * LANES, LANES), LANES)
        value = far_ref[part, :].T
        if step:
            send_refs[step - 1][...] = encode(value)
        else:
            own_ref[...] = value


def gather_lines(own_ref, got_refs, line_ref):
    for step in range(len(got_refs) + 1):
        part = pl.ds(pl.multiple_of((lax.axis_index("yz") ^ step) * LANES, LANES) + PAD, LANES)
        line_ref[part, :] = decode(got_refs[step - 1][...]) if step else own_ref[...]


def column_kernel(table_ref, own_ref, *rest):
    got_refs, (far_ref, line_ref, *scratch) = rest[:-4], rest[-4:]
    gather_lines(own_ref, got_refs, line_ref)
    sparse_pass(line_ref, far_ref, table_ref, *scratch)


def last_kernel(table_ref, outside_ref, own_ref, *rest):
    got_refs, (out_ref, line_ref, far_ref, *scratch, part_ref, sems) = rest[:-7], rest[-7:]
    gather_lines(own_ref, got_refs, line_ref)

    def copy(part):
        return pltpu.make_async_copy(
            part_ref.at[part], out_ref.at[:, pl.ds(part * LANES, LANES)], sems.at[part]
        )

    def finish(part):
        rows = pl.ds(part * LANES, LANES)
        signed = voxel_size * (jnp.sqrt(outside_ref[rows, :]) - jnp.sqrt(far_ref[rows, :]))
        part_ref[part] = signed.T
        copy(part).start()

    dense_pass(line_ref, far_ref, table_ref, *scratch, finish=finish)
    for part in range(LINE // LANES):
        copy(part).wait()


def body(seed_cost, occupied, unknown):
    depth, rows, columns = occupied.shape
    own = depth // lax.axis_size("robot")
    vmem = pl.BlockSpec(memory_space=pltpu.VMEM)
    hbm = pl.BlockSpec(memory_space=pltpu.HBM)
    f32 = jnp.float32

    def call(kernel, out_shape, scratch, *args, source=vmem, target=vmem, limit=16 * 2**20):
        return pl.pallas_call(
            kernel,
            out_shape=out_shape,
            in_specs=[source] * len(args),
            out_specs=jax.tree.map(lambda _: target, out_shape),
            scratch_shapes=scratch,
            compiler_params=pltpu.CompilerParams(vmem_limit_bytes=limit),
            cost_estimate=pl.CostEstimate(flops=4 * 10**6, bytes_accessed=2**20, transcendentals=0),
        )(*args)

    lowest = call(
        lowest_kernel,
        jax.ShapeDtypeStruct(seed_cost.shape[1:], seed_cost.dtype),
        [
            pltpu.VMEM(seed_cost.shape, seed_cost.dtype),
            pltpu.VMEM(seed_cost.shape[1:], seed_cost.dtype),
            pltpu.SemaphoreType.DMA((4,)),
            pltpu.SemaphoreType.DMA((4,)),
        ],
        seed_cost,
        source=hbm,
        target=hbm,
        limit=64 * 2**20 - 400 * 2**10,
    )
    other = lax.ppermute(lowest, "robot", [(0, 1), (1, 0)])
    raised = call(
        prepare_kernel, jax.ShapeDtypeStruct((FIELDS, depth, rows, columns), f32), [], occupied, unknown
    )
    planes = call(
        depth_kernel,
        jax.ShapeDtypeStruct((own, FIELDS, rows, columns), jnp.int16),
        [pltpu.VMEM((FIELDS, depth, rows, columns), f32), pltpu.VMEM((FIELDS, own, rows, columns), f32)],
        lowest,
        other,
        raised,
    )
    crossed = lax.all_to_all(planes, "xy", split_axis=0, concat_axis=0, tiled=True)

    parts = lax.axis_size("yz")
    share = LINE // parts
    line = pltpu.VMEM((LINE + 2 * PAD, LANES), f32)
    scratch = [pltpu.SMEM((BLOCKS,), jnp.int32), pltpu.VMEM((BLOCKS, LANES), f32)]
    lines = [line, pltpu.VMEM((LINE, LANES), f32), *scratch]
    squares = jax.ShapeDtypeStruct((2 * LINE, LANES), f32)
    shapes = (jax.ShapeDtypeStruct((columns, share), f32),)
    shapes += (jax.ShapeDtypeStruct((columns, share), jnp.int16),) * (parts - 1)
    row_calls = [functools.partial(row_kernel, field) for field in range(FIELDS)]
    table, *first = call(row_calls[0], (squares, *shapes), lines, crossed)
    second = call(row_calls[1], shapes, lines, crossed, table)
    settled = []
    for own_part, *others in (first, second):
        got = [
            lax.ppermute(part, "yz", [(i, i ^ step) for i in range(parts)])
            for step, part in enumerate(others, 1)
        ]
        settled.append((own_part, *got))
    outside = call(column_kernel, jax.ShapeDtypeStruct((LINE, share), f32), [line, *scratch], table, *settled[0])
    signed = call(
        last_kernel,
        jax.ShapeDtypeStruct((share, LINE), f32),
        [*lines, pltpu.VMEM((LINE // LANES, share, LANES), f32), pltpu.SemaphoreType.DMA((LINE // LANES,))],
        table,
        outside,
        *settled[1],
        target=hbm,
    )
    return signed[None]


def solution(mesh):
    in_specs = (P("robot", None, "xy", "yz"), P(None, "xy", "yz"), P(None, "xy", "yz"))
    out_specs = P(("robot", "xy"), "yz", None)
    return jax.shard_map(body, mesh=mesh, in_specs=in_specs, out_specs=out_specs, check_vma=False)
```

```python
import functools

import jax
import jax.numpy as jnp
from jax import lax
from jax.experimental import pallas as pl
from jax.experimental.pallas import tpu as pltpu
from jax.sharding import PartitionSpec as P

penalty = 1048576.0
voxel_size = 0.2

LANES = 128
ROWS = 8
LINE = 512
BLOCK = 32
BLOCKS = LINE // BLOCK
GROUPS = BLOCK // ROWS
PAD = ROWS
FIELDS = 2

STEPS = 65520.0 / 13.8629653
HALF_RANGE = 32768


def encode(value):
    code = (jnp.log(1.0 + value) * STEPS + 0.5).astype(jnp.int32)
    return (code - HALF_RANGE).astype(jnp.int16)


def decode(code):
    scaled = (code.astype(jnp.int32) + HALF_RANGE).astype(jnp.float32) * (1.0 / STEPS)
    return jnp.maximum(jnp.exp(scaled) - 1.0, 0.0)


def prepare_kernel(occupied_ref, unknown_ref, raise_ref):
    def masks(place, _):
        taken = occupied_ref[place] == 1
        hidden = taken | (unknown_ref[place] == 1)
        raise_ref[0, place] = jnp.where(taken, 0.0, penalty)
        raise_ref[1, place] = jnp.where(hidden, penalty, 0.0)
        return 0

    lax.fori_loop(0, occupied_ref.shape[0], masks, 0, unroll=4)


def depth_kernel(mine_ref, other_ref, raise_ref, out_ref, field_ref, best_ref):
    half = lax.axis_index("robot")
    depth = mine_ref.shape[0]
    own = out_ref.shape[0]

    def seed(place, _):
        source = place + half * (depth - 1 - 2 * place)
        merged = jnp.minimum(mine_ref[source], other_ref[source]).astype(jnp.float32)
        for field in range(FIELDS):
            field_ref[field, place] = merged + raise_ref[field, source]
        return 0

    lax.fori_loop(0, depth, seed, 0, unroll=8)
    groups = field_ref.shape[2] // ROWS

    def sweep(piece, _):
        field = piece // groups
        rows = pl.ds(pl.multiple_of((piece - field * groups) * ROWS, ROWS), ROWS)
        best = [None] * own
        for source in range(depth):
            value = field_ref[field, source, rows, :]
            for target in range(own):
                candidate = value + float((target - source) ** 2)
                best[target] = candidate if best[target] is None else jnp.minimum(best[target], candidate)
        for target in range(own):
            best_ref[field, target, rows, :] = best[target]
        return 0

    lax.fori_loop(0, FIELDS * groups, sweep, 0)

    def send(target, _):
        place = target + half * (own - 1 - 2 * target)
        for field in range(FIELDS):
            out_ref[place, field] = encode(best_ref[field, target])
        return 0

    lax.fori_loop(0, own, send, 0, unroll=8)


def bit(place):
    return jnp.int32((1 << place) - (1 << 32 if place == 31 else 0))


def find_blocks(line_ref, kept_ref, size, least_gap=0.0, reached_ref=None):
    sublane = lax.broadcasted_iota(jnp.int32, (ROWS, LANES), 0).astype(jnp.float32)
    sources = range(0, LINE, size)
    low = []
    for source in sources:
        least = line_ref[PAD + source : PAD + source + ROWS, :]
        for at in range(PAD + source + ROWS, PAD + source + size, ROWS):
            least = jnp.minimum(least, line_ref[at : at + ROWS, :])
        low.append(jnp.broadcast_to(jnp.min(least, axis=0, keepdims=True), (ROWS, LANES)))
    some = jnp.int32(0)
    for first in range(0, BLOCKS, ROWS):
        bound = jnp.full((ROWS, LANES), penalty, jnp.float32)
        if reached_ref is not None:
            bound = jnp.minimum(bound, reached_ref[first : first + ROWS, :])
        floor = []
        for source, least in zip(sources, low):
            after = sublane * float(BLOCK) + float(first * BLOCK - source)
            far = jnp.maximum(after + float(BLOCK - 1), float(size - 1) - after)
            near = jnp.maximum(jnp.maximum(after - float(size - 1), -after - float(BLOCK - 1)), least_gap)
            bound = jnp.minimum(bound, least + far * far)
            floor.append(least + near * near)
        kept = jnp.zeros((ROWS, 1), jnp.int32)
        for place in range(len(sources)):
            keep = jnp.min(floor[place] - bound, axis=1, keepdims=True) < 0.0
            kept = kept | jnp.where(keep, bit(place), 0)
        for row in range(ROWS):
            word = kept[row, 0]
            kept_ref[first + row] = word
            some = some | jnp.where(word != 0, bit(first + row), 0)
    return some


def lower_block(line_ref, far_ref, table_ref, kept_ref, size, block, start):
    pieces = size // ROWS

    def left(carry):
        return carry[0] != 0

    def pair(carry):
        kept, source, best = carry
        base = pl.multiple_of(block * BLOCK - source * size + LINE, size)
        row = pl.multiple_of(source * size, size) + PAD
        kept = kept ^ lax.shift_left(jnp.int32(1), source)
        best = list(best)
        for p in range(ROWS):
            squares = {k: table_ref[pl.ds(base + (k * ROWS - p), ROWS), :] for k in range(1 - pieces, GROUPS)}
            for q in range(pieces):
                value = jnp.broadcast_to(line_ref[pl.ds(row + q * ROWS + p, 1), :], (ROWS, LANES))
                for group in range(GROUPS):
                    best[group] = jnp.minimum(best[group], value + squares[group - q])
        return kept, 31 - lax.clz(kept), tuple(best)

    kept = kept_ref[block]
    best = lax.while_loop(left, pair, (kept, 31 - lax.clz(kept), start))[2]
    at = pl.multiple_of(block * BLOCK, BLOCK)
    for group in range(GROUPS):
        far_ref[pl.ds(at + group * ROWS, ROWS), :] = best[group]


def fill_table(table_ref):
    sublane = lax.broadcasted_iota(jnp.int32, (ROWS, LANES), 0).astype(jnp.float32)
    for at in range(0, 2 * LINE, ROWS):
        apart = sublane + float(at - LINE)
        table_ref[at : at + ROWS, :] = apart * apart


def sparse_pass(line_ref, far_ref, table_ref, kept_ref, _):
    size = BLOCK // 2
    find_blocks(line_ref, kept_ref, size)

    def target(block, _):
        at = pl.multiple_of(block * BLOCK, BLOCK) + PAD
        start = tuple(line_ref[pl.ds(at + group * ROWS, ROWS), :] for group in range(GROUPS))
        lower_block(line_ref, far_ref, table_ref, kept_ref, size, block, start)
        return 0

    lax.fori_loop(0, BLOCKS, target, 0)


def dense_pass(line_ref, far_ref, table_ref, kept_ref, reached_ref):
    margin = jnp.full((PAD, LANES), 3e38, jnp.float32)
    line_ref[:PAD, :] = margin
    line_ref[PAD + LINE :, :] = margin

    def band(block, _):
        at = pl.multiple_of(block * BLOCK, BLOCK)
        best = [None] * GROUPS
        for p in range(ROWS):
            first = LINE - p
            squares = {k: table_ref[first + k * ROWS : first + (k + 1) * ROWS, :] for k in (-1, 0, 1)}
            for q in range(-1, GROUPS + 1):
                value = jnp.broadcast_to(line_ref[pl.ds(at + (PAD + q * ROWS + p), 1), :], (ROWS, LANES))
                for group in range(max(q - 1, 0), min(q + 2, GROUPS)):
                    candidate = value + squares[group - q]
                    best[group] = candidate if best[group] is None else jnp.minimum(best[group], candidate)
        most = best[0]
        for group in range(GROUPS):
            far_ref[pl.ds(at + group * ROWS, ROWS), :] = best[group]
            most = jnp.maximum(most, best[group])
        reached_ref[pl.ds(block, 1), :] = jnp.max(most, axis=0, keepdims=True)
        return 0

    lax.fori_loop(0, BLOCKS, band, 0, unroll=2)

    def left(some):
        return some != 0

    def target(some):
        block = 31 - lax.clz(some)
        at = pl.multiple_of(block * BLOCK, BLOCK)
        start = tuple(far_ref[pl.ds(at + group * ROWS, ROWS), :] for group in range(GROUPS))
        lower_block(line_ref, far_ref, table_ref, kept_ref, BLOCK, block, start)
        return some ^ lax.shift_left(jnp.int32(1), block)

    lax.while_loop(left, target, find_blocks(line_ref, kept_ref, BLOCK, float(ROWS + 1), reached_ref))


PASSES = (sparse_pass, dense_pass)


def row_kernel(field, in_ref, table_ref, own_ref, *rest):
    send_refs, (line_ref, far_ref, *scratch) = rest[:-4], rest[-4:]
    chunk = in_ref.shape[2]
    if field == 0:
        fill_table(table_ref)
    for piece in range(in_ref.shape[0]):
        line_ref[PAD + piece * chunk : PAD + (piece + 1) * chunk, :] = decode(in_ref[piece, field])
    PASSES[field](line_ref, far_ref, table_ref, *scratch)
    for step in range(len(send_refs) + 1):
        part = pl.ds(pl.multiple_of((lax.axis_index("yz") ^ step) * LANES, LANES), LANES)
        value = far_ref[part, :].T
        if step:
            send_refs[step - 1][...] = encode(value)
        else:
            own_ref[...] = value


def gather_lines(own_ref, got_refs, line_ref):
    for step in range(len(got_refs) + 1):
        part = pl.ds(pl.multiple_of((lax.axis_index("yz") ^ step) * LANES, LANES) + PAD, LANES)
        line_ref[part, :] = decode(got_refs[step - 1][...]) if step else own_ref[...]


def column_kernel(table_ref, own_ref, *rest):
    got_refs, (far_ref, line_ref, *scratch) = rest[:-4], rest[-4:]
    gather_lines(own_ref, got_refs, line_ref)
    sparse_pass(line_ref, far_ref, table_ref, *scratch)


def last_kernel(table_ref, outside_ref, own_ref, *rest):
    got_refs, (out_ref, line_ref, far_ref, *scratch) = rest[:-5], rest[-5:]
    gather_lines(own_ref, got_refs, line_ref)
    dense_pass(line_ref, far_ref, table_ref, *scratch)
    for piece in range(LINE // LANES):
        part = pl.ds(piece * LANES, LANES)
        signed = voxel_size * (jnp.sqrt(outside_ref[part, :]) - jnp.sqrt(far_ref[part, :]))
        out_ref[:, part] = signed.T


def body(seed_cost, occupied, unknown):
    depth, rows, columns = occupied.shape
    own = depth // lax.axis_size("robot")
    vmem = pl.BlockSpec(memory_space=pltpu.VMEM)
    f32 = jnp.float32

    def call(kernel, out_shape, scratch, *args):
        return pl.pallas_call(
            kernel,
            out_shape=out_shape,
            in_specs=[vmem] * len(args),
            out_specs=jax.tree.map(lambda _: vmem, out_shape),
            scratch_shapes=scratch,
            compiler_params=pltpu.CompilerParams(vmem_limit_bytes=16 * 2**20),
            cost_estimate=pl.CostEstimate(flops=4 * 10**6, bytes_accessed=2**20, transcendentals=0),
        )(*args)

    lowest = jnp.min(seed_cost, axis=0)
    other = lax.ppermute(lowest, "robot", [(0, 1), (1, 0)])
    raised = call(
        prepare_kernel, jax.ShapeDtypeStruct((FIELDS, depth, rows, columns), f32), [], occupied, unknown
    )
    planes = call(
        depth_kernel,
        jax.ShapeDtypeStruct((own, FIELDS, rows, columns), jnp.int16),
        [pltpu.VMEM((FIELDS, depth, rows, columns), f32), pltpu.VMEM((FIELDS, own, rows, columns), f32)],
        lowest,
        other,
        raised,
    )
    crossed = lax.all_to_all(planes, "xy", split_axis=0, concat_axis=0, tiled=True)

    parts = lax.axis_size("yz")
    share = LINE // parts
    line = pltpu.VMEM((LINE + 2 * PAD, LANES), f32)
    scratch = [pltpu.SMEM((BLOCKS,), jnp.int32), pltpu.VMEM((BLOCKS, LANES), f32)]
    lines = [line, pltpu.VMEM((LINE, LANES), f32), *scratch]
    squares = jax.ShapeDtypeStruct((2 * LINE, LANES), f32)
    shapes = (jax.ShapeDtypeStruct((columns, share), f32),)
    shapes += (jax.ShapeDtypeStruct((columns, share), jnp.int16),) * (parts - 1)
    row_calls = [functools.partial(row_kernel, field) for field in range(FIELDS)]
    table, *first = call(row_calls[0], (squares, *shapes), lines, crossed)
    second = call(row_calls[1], shapes, lines, crossed, table)
    settled = []
    for own_part, *others in (first, second):
        got = [
            lax.ppermute(part, "yz", [(i, i ^ step) for i in range(parts)])
            for step, part in enumerate(others, 1)
        ]
        settled.append((own_part, *got))
    outside = call(column_kernel, jax.ShapeDtypeStruct((LINE, share), f32), [line, *scratch], table, *settled[0])
    signed = call(
        last_kernel,
        jax.ShapeDtypeStruct((share, LINE), f32),
        lines,
        table,
        outside,
        *settled[1],
    )
    return signed[None]


def solution(mesh):
    in_specs = (P("robot", None, "xy", "yz"), P(None, "xy", "yz"), P(None, "xy", "yz"))
    out_specs = P(("robot", "xy"), "yz", None)
    return jax.shard_map(body, mesh=mesh, in_specs=in_specs, out_specs=out_specs, check_vma=False)
```

```python
import functools

import jax
import jax.numpy as jnp
from jax import lax
from jax.experimental import pallas as pl
from jax.experimental.pallas import tpu as pltpu
from jax.sharding import PartitionSpec as P

penalty = 1048576.0
voxel_size = 0.2

LANES = 128
ROWS = 8
LINE = 512
BLOCK = 32
BLOCKS = LINE // BLOCK
GROUPS = BLOCK // ROWS
PAD = ROWS
FIELDS = 2

STEPS = 65520.0 / 13.8629653
HALF_RANGE = 32768


def encode(value):
    code = (jnp.log(1.0 + value) * STEPS + 0.5).astype(jnp.int32)
    return (code - HALF_RANGE).astype(jnp.int16)


def decode(code):
    scaled = (code.astype(jnp.int32) + HALF_RANGE).astype(jnp.float32) * (1.0 / STEPS)
    return jnp.maximum(jnp.exp(scaled) - 1.0, 0.0)


def prepare_kernel(occupied_ref, unknown_ref, raise_ref):
    def masks(place, _):
        taken = occupied_ref[place] == 1
        hidden = taken | (unknown_ref[place] == 1)
        raise_ref[0, place] = jnp.where(taken, 0.0, penalty)
        raise_ref[1, place] = jnp.where(hidden, penalty, 0.0)
        return 0

    lax.fori_loop(0, occupied_ref.shape[0], masks, 0, unroll=4)


def depth_kernel(mine_ref, other_ref, raise_ref, out_ref, field_ref, best_ref):
    half = lax.axis_index("robot")
    depth = mine_ref.shape[0]
    own = out_ref.shape[0]

    def seed(place, _):
        source = place + half * (depth - 1 - 2 * place)
        merged = jnp.minimum(mine_ref[source], other_ref[source]).astype(jnp.float32)
        for field in range(FIELDS):
            field_ref[field, place] = merged + raise_ref[field, source]
        return 0

    lax.fori_loop(0, depth, seed, 0, unroll=8)
    groups = field_ref.shape[2] // ROWS

    def sweep(piece, _):
        field = piece // groups
        rows = pl.ds(pl.multiple_of((piece - field * groups) * ROWS, ROWS), ROWS)
        best = [None] * own
        for source in range(depth):
            value = field_ref[field, source, rows, :]
            for target in range(own):
                candidate = value + float((target - source) ** 2)
                best[target] = candidate if best[target] is None else jnp.minimum(best[target], candidate)
        for target in range(own):
            best_ref[field, target, rows, :] = best[target]
        return 0

    lax.fori_loop(0, FIELDS * groups, sweep, 0)

    def send(target, _):
        place = target + half * (own - 1 - 2 * target)
        for field in range(FIELDS):
            out_ref[place, field] = encode(best_ref[field, target])
        return 0

    lax.fori_loop(0, own, send, 0, unroll=8)


def bit(place):
    return jnp.int32((1 << place) - (1 << 32 if place == 31 else 0))


def find_blocks(line_ref, kept_ref, size, least_gap=0.0, reached_ref=None):
    sublane = lax.broadcasted_iota(jnp.int32, (ROWS, LANES), 0).astype(jnp.float32)
    sources = range(0, LINE, size)
    low = []
    for source in sources:
        least = line_ref[PAD + source : PAD + source + ROWS, :]
        for at in range(PAD + source + ROWS, PAD + source + size, ROWS):
            least = jnp.minimum(least, line_ref[at : at + ROWS, :])
        low.append(jnp.broadcast_to(jnp.min(least, axis=0, keepdims=True), (ROWS, LANES)))
    some = jnp.int32(0)
    for first in range(0, BLOCKS, ROWS):
        bound = jnp.full((ROWS, LANES), penalty, jnp.float32)
        if reached_ref is not None:
            bound = jnp.minimum(bound, reached_ref[first : first + ROWS, :])
        floor = []
        for source, least in zip(sources, low):
            after = sublane * float(BLOCK) + float(first * BLOCK - source)
            far = jnp.maximum(after + float(BLOCK - 1), float(size - 1) - after)
            near = jnp.maximum(jnp.maximum(after - float(size - 1), -after - float(BLOCK - 1)), least_gap)
            bound = jnp.minimum(bound, least + far * far)
            floor.append(least + near * near)
        kept = jnp.zeros((ROWS, 1), jnp.int32)
        for place in range(len(sources)):
            keep = jnp.min(floor[place] - bound, axis=1, keepdims=True) < 0.0
            kept = kept | jnp.where(keep, bit(place), 0)
        for row in range(ROWS):
            word = kept[row, 0]
            kept_ref[first + row] = word
            some = some | jnp.where(word != 0, bit(first + row), 0)
    return some


def lower_block(line_ref, far_ref, table_ref, kept_ref, size, block, start):
    pieces = size // ROWS

    def left(carry):
        return carry[0] != 0

    def pair(carry):
        kept, source, best = carry
        base = pl.multiple_of(block * BLOCK - source * size + LINE, size)
        row = pl.multiple_of(source * size, size) + PAD
        kept = kept ^ lax.shift_left(jnp.int32(1), source)
        best = list(best)
        for p in range(ROWS):
            squares = {k: table_ref[pl.ds(base + (k * ROWS - p), ROWS), :] for k in range(1 - pieces, GROUPS)}
            for q in range(pieces):
                value = jnp.broadcast_to(line_ref[pl.ds(row + q * ROWS + p, 1), :], (ROWS, LANES))
                for group in range(GROUPS):
                    best[group] = jnp.minimum(best[group], value + squares[group - q])
        return kept, 31 - lax.clz(kept), tuple(best)

    kept = kept_ref[block]
    best = lax.while_loop(left, pair, (kept, 31 - lax.clz(kept), start))[2]
    at = pl.multiple_of(block * BLOCK, BLOCK)
    for group in range(GROUPS):
        far_ref[pl.ds(at + group * ROWS, ROWS), :] = best[group]


def fill_table(table_ref):
    sublane = lax.broadcasted_iota(jnp.int32, (ROWS, LANES), 0).astype(jnp.float32)
    for at in range(0, 2 * LINE, ROWS):
        apart = sublane + float(at - LINE)
        table_ref[at : at + ROWS, :] = apart * apart


def sparse_pass(line_ref, far_ref, table_ref, kept_ref, _):
    size = BLOCK // 2
    find_blocks(line_ref, kept_ref, size)

    def target(block, _):
        at = pl.multiple_of(block * BLOCK, BLOCK) + PAD
        start = tuple(line_ref[pl.ds(at + group * ROWS, ROWS), :] for group in range(GROUPS))
        lower_block(line_ref, far_ref, table_ref, kept_ref, size, block, start)
        return 0

    lax.fori_loop(0, BLOCKS, target, 0)


def dense_pass(line_ref, far_ref, table_ref, kept_ref, reached_ref):
    margin = jnp.full((PAD, LANES), 3e38, jnp.float32)
    line_ref[:PAD, :] = margin
    line_ref[PAD + LINE : 2 * PAD + LINE, :] = margin

    def band(block, _):
        at = pl.multiple_of(block * BLOCK, BLOCK)
        best = [None] * GROUPS
        for p in range(ROWS):
            first = LINE - p
            squares = {k: table_ref[first + k * ROWS : first + (k + 1) * ROWS, :] for k in (-1, 0, 1)}
            for q in range(-1, GROUPS + 1):
                value = jnp.broadcast_to(line_ref[pl.ds(at + (PAD + q * ROWS + p), 1), :], (ROWS, LANES))
                for group in range(max(q - 1, 0), min(q + 2, GROUPS)):
                    candidate = value + squares[group - q]
                    best[group] = candidate if best[group] is None else jnp.minimum(best[group], candidate)
        most = best[0]
        for group in range(GROUPS):
            far_ref[pl.ds(at + group * ROWS, ROWS), :] = best[group]
            most = jnp.maximum(most, best[group])
        reached_ref[pl.ds(block, 1), :] = jnp.max(most, axis=0, keepdims=True)
        return 0

    lax.fori_loop(0, BLOCKS, band, 0, unroll=2)

    def left(some):
        return some != 0

    def target(some):
        block = 31 - lax.clz(some)
        at = pl.multiple_of(block * BLOCK, BLOCK)
        start = tuple(far_ref[pl.ds(at + group * ROWS, ROWS), :] for group in range(GROUPS))
        lower_block(line_ref, far_ref, table_ref, kept_ref, BLOCK, block, start)
        return some ^ lax.shift_left(jnp.int32(1), block)

    lax.while_loop(left, target, find_blocks(line_ref, kept_ref, BLOCK, float(ROWS + 1), reached_ref))


PASSES = (sparse_pass, dense_pass)


def row_kernel(field, in_ref, table_ref, own_ref, *rest):
    send_refs, (line_ref, far_ref, *scratch) = rest[:-4], rest[-4:]
    chunk = in_ref.shape[2]
    if field == 0:
        fill_table(table_ref)
    for piece in range(in_ref.shape[0]):
        line_ref[PAD + piece * chunk : PAD + (piece + 1) * chunk, :] = decode(in_ref[piece, field])
    PASSES[field](line_ref, far_ref, table_ref, *scratch)
    for step in range(len(send_refs) + 1):
        part = pl.ds(pl.multiple_of((lax.axis_index("yz") ^ step) * LANES, LANES), LANES)
        value = far_ref[part, :].T
        if step:
            send_refs[step - 1][...] = encode(value)
        else:
            own_ref[...] = value


def gather_lines(own_ref, got_refs, line_ref):
    for step in range(len(got_refs) + 1):
        part = pl.ds(pl.multiple_of((lax.axis_index("yz") ^ step) * LANES, LANES) + PAD, LANES)
        line_ref[part, :] = decode(got_refs[step - 1][...]) if step else own_ref[...]


def column_kernel(table_ref, own_ref, *rest):
    got_refs, (far_ref, line_ref, *scratch) = rest[:-4], rest[-4:]
    gather_lines(own_ref, got_refs, line_ref)
    sparse_pass(line_ref, far_ref, table_ref, *scratch)


def last_kernel(table_ref, outside_ref, own_ref, *rest):
    got_refs, (out_ref, line_ref, far_ref, *scratch) = rest[:-5], rest[-5:]
    gather_lines(own_ref, got_refs, line_ref)
    dense_pass(line_ref, far_ref, table_ref, *scratch)
    for piece in range(LINE // LANES):
        part = pl.ds(piece * LANES, LANES)
        signed = voxel_size * (jnp.sqrt(outside_ref[part, :]) - jnp.sqrt(far_ref[part, :]))
        out_ref[:, part] = signed.T


def body(seed_cost, occupied, unknown):
    depth, rows, columns = occupied.shape
    own = depth // lax.axis_size("robot")
    vmem = pl.BlockSpec(memory_space=pltpu.VMEM)
    f32 = jnp.float32

    def call(kernel, out_shape, scratch, *args):
        return pl.pallas_call(
            kernel,
            out_shape=out_shape,
            in_specs=[vmem] * len(args),
            out_specs=jax.tree.map(lambda _: vmem, out_shape),
            scratch_shapes=scratch,
            compiler_params=pltpu.CompilerParams(vmem_limit_bytes=16 * 2**20),
            cost_estimate=pl.CostEstimate(flops=4 * 10**6, bytes_accessed=2**20, transcendentals=0),
        )(*args)

    lowest = jnp.min(seed_cost, axis=0)
    other = lax.ppermute(lowest, "robot", [(0, 1), (1, 0)])
    raised = call(
        prepare_kernel, jax.ShapeDtypeStruct((FIELDS, depth, rows, columns), f32), [], occupied, unknown
    )
    planes = call(
        depth_kernel,
        jax.ShapeDtypeStruct((own, FIELDS, rows, columns), jnp.int16),
        [pltpu.VMEM((FIELDS, depth, rows, columns), f32), pltpu.VMEM((FIELDS, own, rows, columns), f32)],
        lowest,
        other,
        raised,
    )
    crossed = lax.all_to_all(planes, "xy", split_axis=0, concat_axis=0, tiled=True)

    parts = lax.axis_size("yz")
    share = LINE // parts
    line = pltpu.VMEM((LINE + 2 * PAD + ROWS, LANES), f32)
    scratch = [pltpu.SMEM((BLOCKS,), jnp.int32), pltpu.VMEM((BLOCKS + ROWS, LANES), f32)]
    lines = [line, pltpu.VMEM((LINE, LANES), f32), *scratch]
    squares = jax.ShapeDtypeStruct((2 * LINE, LANES), f32)
    shapes = (jax.ShapeDtypeStruct((columns, share), f32),)
    shapes += (jax.ShapeDtypeStruct((columns, share), jnp.int16),) * (parts - 1)
    row_calls = [functools.partial(row_kernel, field) for field in range(FIELDS)]
    table, *first = call(row_calls[0], (squares, *shapes), lines, crossed)
    second = call(row_calls[1], shapes, lines, crossed, table)
    settled = []
    for own_part, *others in (first, second):
        got = [
            lax.ppermute(part, "yz", [(i, i ^ step) for i in range(parts)])
            for step, part in enumerate(others, 1)
        ]
        settled.append((own_part, *got))
    outside = call(column_kernel, jax.ShapeDtypeStruct((LINE, share), f32), [line, *scratch], table, *settled[0])
    signed = call(
        last_kernel,
        jax.ShapeDtypeStruct((share, LINE), f32),
        lines,
        table,
        outside,
        *settled[1],
    )
    return signed[None]


def solution(mesh):
    in_specs = (P("robot", None, "xy", "yz"), P(None, "xy", "yz"), P(None, "xy", "yz"))
    out_specs = P(("robot", "xy"), "yz", None)
    return jax.shard_map(body, mesh=mesh, in_specs=in_specs, out_specs=out_specs, check_vma=False)
```

```python
import functools

import jax
import jax.numpy as jnp
from jax import lax
from jax.experimental import pallas as pl
from jax.experimental.pallas import tpu as pltpu
from jax.sharding import PartitionSpec as P

penalty = 1048576.0
voxel_size = 0.2

LANES = 128
ROWS = 8
LINE = 512
BLOCK = 32
BLOCKS = LINE // BLOCK
GROUPS = BLOCK // ROWS
FINE = BLOCK // 2
PAD = ROWS
FIELDS = 2

STEPS = 65520.0 / 13.8629653
HALF_RANGE = 32768


def encode(value):
    code = (jnp.log(1.0 + value) * STEPS + 0.5).astype(jnp.int32)
    return (code - HALF_RANGE).astype(jnp.int16)


def decode(code):
    scaled = (code.astype(jnp.int32) + HALF_RANGE).astype(jnp.float32) * (1.0 / STEPS)
    return jnp.maximum(jnp.exp(scaled) - 1.0, 0.0)


def prepare_kernel(occupied_ref, unknown_ref, raise_ref, table_ref, spans_ref):
    def masks(place, _):
        taken = occupied_ref[place] == 1
        hidden = taken | (unknown_ref[place] == 1)
        raise_ref[0, place] = jnp.where(taken, 0.0, penalty)
        raise_ref[1, place] = jnp.where(hidden, penalty, 0.0)
        return 0

    lax.fori_loop(0, occupied_ref.shape[0], masks, 0, unroll=4)
    fill_table(table_ref)
    for half in range(BLOCKS // ROWS):
        for place in range(LINE // FINE):
            for kind, squares in enumerate(spans(half * ROWS, place * FINE, FINE, 0.0)):
                spans_ref[kind, half, place] = squares


def depth_kernel(mine_ref, other_ref, raise_ref, out_ref, field_ref, best_ref):
    half = lax.axis_index("robot")
    depth = mine_ref.shape[0]
    own = out_ref.shape[0]

    def seed(place, _):
        source = place + half * (depth - 1 - 2 * place)
        merged = jnp.minimum(mine_ref[source], other_ref[source]).astype(jnp.float32)
        for field in range(FIELDS):
            field_ref[field, place] = merged + raise_ref[field, source]
        return 0

    lax.fori_loop(0, depth, seed, 0, unroll=8)
    groups = field_ref.shape[2] // ROWS

    def sweep(piece, _):
        field = piece // groups
        rows = pl.ds(pl.multiple_of((piece - field * groups) * ROWS, ROWS), ROWS)
        best = [None] * own
        for source in range(depth):
            value = field_ref[field, source, rows, :]
            for target in range(own):
                candidate = value + float((target - source) ** 2)
                best[target] = candidate if best[target] is None else jnp.minimum(best[target], candidate)
        for target in range(own):
            best_ref[field, target, rows, :] = best[target]
        return 0

    lax.fori_loop(0, FIELDS * groups, sweep, 0)

    def send(target, _):
        place = target + half * (own - 1 - 2 * target)
        for field in range(FIELDS):
            out_ref[place, field] = encode(best_ref[field, target])
        return 0

    lax.fori_loop(0, own, send, 0, unroll=8)


def bit(place):
    return jnp.int32((1 << place) - (1 << 32 if place == 31 else 0))


def spans(first, source, size, least_gap):
    sublane = lax.broadcasted_iota(jnp.int32, (ROWS, LANES), 0).astype(jnp.float32)
    after = sublane * float(BLOCK) + float(first * BLOCK - source)
    far = jnp.maximum(after + float(BLOCK - 1), float(size - 1) - after)
    near = jnp.maximum(jnp.maximum(after - float(size - 1), -after - float(BLOCK - 1)), least_gap)
    return far * far, near * near


def find_blocks(line_ref, kept_ref, size, least_gap=0.0, reached_ref=None, spans_ref=None):
    sources = range(0, LINE, size)
    low = []
    for source in sources:
        least = line_ref[PAD + source : PAD + source + ROWS, :]
        for at in range(PAD + source + ROWS, PAD + source + size, ROWS):
            least = jnp.minimum(least, line_ref[at : at + ROWS, :])
        low.append(jnp.broadcast_to(jnp.min(least, axis=0, keepdims=True), (ROWS, LANES)))
    some = jnp.int32(0)
    for first in range(0, BLOCKS, ROWS):
        bound = jnp.full((ROWS, LANES), penalty, jnp.float32)
        if reached_ref is not None:
            bound = jnp.minimum(bound, reached_ref[first : first + ROWS, :])
        floor = []
        for place, (source, least) in enumerate(zip(sources, low)):
            if spans_ref is None:
                far, near = spans(first, source, size, least_gap)
            else:
                far, near = (spans_ref[kind, first // ROWS, place] for kind in range(2))
            bound = jnp.minimum(bound, least + far)
            floor.append(least + near)
        kept = jnp.zeros((ROWS, 1), jnp.int32)
        for place in range(len(sources)):
            keep = jnp.min(floor[place] - bound, axis=1, keepdims=True) < 0.0
            kept = kept | jnp.where(keep, bit(place), 0)
        for row in range(ROWS):
            word = kept[row, 0]
            kept_ref[first + row] = word
            some = some | jnp.where(word != 0, bit(first + row), 0)
    return some


def lower_block(line_ref, far_ref, table_ref, kept_ref, size, block, start):
    pieces = size // ROWS

    def left(carry):
        return carry[0] != 0

    def pair(carry):
        kept, source, best = carry
        base = pl.multiple_of(block * BLOCK - source * size + LINE, size)
        row = pl.multiple_of(source * size, size) + PAD
        kept = kept ^ lax.shift_left(jnp.int32(1), source)
        best = list(best)
        for p in range(ROWS):
            squares = {k: table_ref[pl.ds(base + (k * ROWS - p), ROWS), :] for k in range(1 - pieces, GROUPS)}
            for q in range(pieces):
                value = jnp.broadcast_to(line_ref[pl.ds(row + q * ROWS + p, 1), :], (ROWS, LANES))
                for group in range(GROUPS):
                    best[group] = jnp.minimum(best[group], value + squares[group - q])
        return kept, 31 - lax.clz(kept), tuple(best)

    kept = kept_ref[block]
    best = lax.while_loop(left, pair, (kept, 31 - lax.clz(kept), start))[2]
    at = pl.multiple_of(block * BLOCK, BLOCK)
    for group in range(GROUPS):
        far_ref[pl.ds(at + group * ROWS, ROWS), :] = best[group]


def fill_table(table_ref):
    sublane = lax.broadcasted_iota(jnp.int32, (ROWS, LANES), 0).astype(jnp.float32)
    for at in range(0, 2 * LINE, ROWS):
        apart = sublane + float(at - LINE)
        table_ref[at : at + ROWS, :] = apart * apart


def sparse_pass(line_ref, far_ref, table_ref, spans_ref, kept_ref, _):
    size = FINE
    find_blocks(line_ref, kept_ref, size, spans_ref=spans_ref)

    def target(block, _):
        at = pl.multiple_of(block * BLOCK, BLOCK) + PAD
        start = tuple(line_ref[pl.ds(at + group * ROWS, ROWS), :] for group in range(GROUPS))
        lower_block(line_ref, far_ref, table_ref, kept_ref, size, block, start)
        return 0

    lax.fori_loop(0, BLOCKS, target, 0)


def dense_pass(line_ref, far_ref, table_ref, _, kept_ref, reached_ref):
    margin = jnp.full((PAD, LANES), 3e38, jnp.float32)
    line_ref[:PAD, :] = margin
    line_ref[PAD + LINE : 2 * PAD + LINE, :] = margin

    def band(block, _):
        at = pl.multiple_of(block * BLOCK, BLOCK)
        best = [None] * GROUPS
        for p in range(ROWS):
            first = LINE - p
            squares = {k: table_ref[first + k * ROWS : first + (k + 1) * ROWS, :] for k in (-1, 0, 1)}
            for q in range(-1, GROUPS + 1):
                value = jnp.broadcast_to(line_ref[pl.ds(at + (PAD + q * ROWS + p), 1), :], (ROWS, LANES))
                for group in range(max(q - 1, 0), min(q + 2, GROUPS)):
                    candidate = value + squares[group - q]
                    best[group] = candidate if best[group] is None else jnp.minimum(best[group], candidate)
        most = best[0]
        for group in range(GROUPS):
            far_ref[pl.ds(at + group * ROWS, ROWS), :] = best[group]
            most = jnp.maximum(most, best[group])
        reached_ref[pl.ds(block, 1), :] = jnp.max(most, axis=0, keepdims=True)
        return 0

    lax.fori_loop(0, BLOCKS, band, 0, unroll=2)

    def left(some):
        return some != 0

    def target(some):
        block = 31 - lax.clz(some)
        at = pl.multiple_of(block * BLOCK, BLOCK)
        start = tuple(far_ref[pl.ds(at + group * ROWS, ROWS), :] for group in range(GROUPS))
        lower_block(line_ref, far_ref, table_ref, kept_ref, BLOCK, block, start)
        return some ^ lax.shift_left(jnp.int32(1), block)

    lax.while_loop(left, target, find_blocks(line_ref, kept_ref, BLOCK, float(ROWS + 1), reached_ref))


PASSES = (sparse_pass, dense_pass)


def row_kernel(field, in_ref, table_ref, spans_ref, own_ref, *rest):
    send_refs, (line_ref, far_ref, *scratch) = rest[:-4], rest[-4:]
    chunk = in_ref.shape[2]
    for piece in range(in_ref.shape[0]):
        line_ref[PAD + piece * chunk : PAD + (piece + 1) * chunk, :] = decode(in_ref[piece, field])
    PASSES[field](line_ref, far_ref, table_ref, spans_ref, *scratch)
    for step in range(len(send_refs) + 1):
        part = pl.ds(pl.multiple_of((lax.axis_index("yz") ^ step) * LANES, LANES), LANES)
        value = far_ref[part, :].T
        if step:
            send_refs[step - 1][...] = encode(value)
        else:
            own_ref[...] = value


def gather_lines(own_ref, got_refs, line_ref):
    for step in range(len(got_refs) + 1):
        part = pl.ds(pl.multiple_of((lax.axis_index("yz") ^ step) * LANES, LANES) + PAD, LANES)
        line_ref[part, :] = decode(got_refs[step - 1][...]) if step else own_ref[...]


def column_kernel(table_ref, spans_ref, own_ref, *rest):
    got_refs, (far_ref, line_ref, *scratch) = rest[:-4], rest[-4:]
    gather_lines(own_ref, got_refs, line_ref)
    sparse_pass(line_ref, far_ref, table_ref, spans_ref, *scratch)


def last_kernel(table_ref, outside_ref, own_ref, *rest):
    got_refs, (out_ref, line_ref, far_ref, *scratch) = rest[:-5], rest[-5:]
    gather_lines(own_ref, got_refs, line_ref)
    dense_pass(line_ref, far_ref, table_ref, None, *scratch)
    for piece in range(LINE // LANES):
        part = pl.ds(piece * LANES, LANES)
        signed = voxel_size * (jnp.sqrt(outside_ref[part, :]) - jnp.sqrt(far_ref[part, :]))
        out_ref[:, part] = signed.T


def body(seed_cost, occupied, unknown):
    depth, rows, columns = occupied.shape
    own = depth // lax.axis_size("robot")
    vmem = pl.BlockSpec(memory_space=pltpu.VMEM)
    f32 = jnp.float32

    def call(kernel, out_shape, scratch, *args):
        return pl.pallas_call(
            kernel,
            out_shape=out_shape,
            in_specs=[vmem] * len(args),
            out_specs=jax.tree.map(lambda _: vmem, out_shape),
            scratch_shapes=scratch,
            compiler_params=pltpu.CompilerParams(vmem_limit_bytes=16 * 2**20),
            cost_estimate=pl.CostEstimate(flops=4 * 10**6, bytes_accessed=2**20, transcendentals=0),
        )(*args)

    lowest = jnp.min(seed_cost, axis=0)
    other = lax.ppermute(lowest, "robot", [(0, 1), (1, 0)])
    raised, table, squares = call(
        prepare_kernel,
        (
            jax.ShapeDtypeStruct((FIELDS, depth, rows, columns), f32),
            jax.ShapeDtypeStruct((2 * LINE, LANES), f32),
            jax.ShapeDtypeStruct((2, BLOCKS // ROWS, LINE // FINE, ROWS, LANES), f32),
        ),
        [],
        occupied,
        unknown,
    )
    planes = call(
        depth_kernel,
        jax.ShapeDtypeStruct((own, FIELDS, rows, columns), jnp.int16),
        [pltpu.VMEM((FIELDS, depth, rows, columns), f32), pltpu.VMEM((FIELDS, own, rows, columns), f32)],
        lowest,
        other,
        raised,
    )
    crossed = lax.all_to_all(planes, "xy", split_axis=0, concat_axis=0, tiled=True)

    parts = lax.axis_size("yz")
    share = LINE // parts
    line = pltpu.VMEM((LINE + 2 * PAD + ROWS, LANES), f32)
    scratch = [pltpu.SMEM((BLOCKS,), jnp.int32), pltpu.VMEM((BLOCKS + ROWS, LANES), f32)]
    lines = [line, pltpu.VMEM((LINE, LANES), f32), *scratch]
    shapes = (jax.ShapeDtypeStruct((columns, share), f32),)
    shapes += (jax.ShapeDtypeStruct((columns, share), jnp.int16),) * (parts - 1)
    settled = []
    for field in range(FIELDS):
        own_part, *others = call(functools.partial(row_kernel, field), shapes, lines, crossed, table, squares)
        got = [
            lax.ppermute(part, "yz", [(i, i ^ step) for i in range(parts)])
            for step, part in enumerate(others, 1)
        ]
        settled.append((own_part, *got))
    outside = call(column_kernel, jax.ShapeDtypeStruct((LINE, share), f32), [line, *scratch], table, squares, *settled[0])
    signed = call(
        last_kernel,
        jax.ShapeDtypeStruct((share, LINE), f32),
        lines,
        table,
        outside,
        *settled[1],
    )
    return signed[None]


def solution(mesh):
    in_specs = (P("robot", None, "xy", "yz"), P(None, "xy", "yz"), P(None, "xy", "yz"))
    out_specs = P(("robot", "xy"), "yz", None)
    return jax.shard_map(body, mesh=mesh, in_specs=in_specs, out_specs=out_specs, check_vma=False)
```
